32 devices in a mesh: fsdp: 2 (over y), ctx: 4 (over z), tp: 4 (over x, core).
Axes of the slice: x: 2, y: 2, z: 4, core: 2. Of those that a mesh axis runs over, the one named last changes fastest.
Arguments:
- tokens: bfloat16 [4, 512, 768], P('fsdp', 'ctx'), may hold values from -10 to 10
- lengths: int32 [4, 6], P('fsdp'), may hold values from 1 to 320, 512 in all within a row
- qkv_weight: bfloat16 [3, 768, 768], P(None, ('fsdp', 'ctx'), 'tp')
- qv_bias: bfloat16 [2, 12, 64], P(None, 'tp', ('fsdp', 'ctx')), may hold values from -3 to 3
- out_weight: bfloat16 [768, 768], P('tp', ('fsdp', 'ctx')), may hold values from -0.875 to 0.875
- out_bias: bfloat16 [768], P(('fsdp', 'ctx')), may hold values from -3 to 3
- norm1_gain: bfloat16 [768], P(('fsdp', 'ctx')), may hold values from 0.099609375 to 1.8984375
- norm1_bias: bfloat16 [768], P(('fsdp', 'ctx')), may hold values from -3 to 3
- up_weight: bfloat16 [768, 3072], P(('fsdp', 'ctx'), 'tp'), may hold values from -0.21875 to 0.21875
- up_bias: bfloat16 [48, 64], P('tp', ('fsdp', 'ctx')), may hold values from -3 to 3
- down_weight: bfloat16 [3072, 768], P('tp', ('fsdp', 'ctx')), may hold values from -0.109375 to 0.109375
- down_bias: bfloat16 [768], P(('fsdp', 'ctx')), may hold values from -3 to 3
- norm2_gain: bfloat16 [768], P(('fsdp', 'ctx')), may hold values from 0.099609375 to 1.8984375
- norm2_bias: bfloat16 [768], P(('fsdp', 'ctx')), may hold values from -3 to 3
- cotangent: bfloat16 [4, 512, 768], P('fsdp', 'ctx'), may hold values from -6 to 6
Outputs:
- output: bfloat16 [4, 512, 768], P('fsdp', 'ctx')
- tokens_grad: bfloat16 [4, 512, 768], P('fsdp', 'ctx')
- qkv_weight_grad: float32 [3, 768, 768], P(None, ('fsdp', 'ctx'), 'tp')
- qv_bias_grad: float32 [2, 12, 64], P(None, 'tp', ('fsdp', 'ctx'))
- out_weight_grad: float32 [768, 768], P('tp', ('fsdp', 'ctx'))
- out_bias_grad: float32 [768], P(('fsdp', 'ctx'))
- norm1_gain_grad: float32 [768], P(('fsdp', 'ctx'))
- norm1_bias_grad: float32 [768], P(('fsdp', 'ctx'))
- up_weight_grad: float32 [768, 3072], P(('fsdp', 'ctx'), 'tp')
- up_bias_grad: float32 [48, 64], P('tp', ('fsdp', 'ctx'))
- down_weight_grad: float32 [3072, 768], P('tp', ('fsdp', 'ctx'))
- down_bias_grad: float32 [768], P(('fsdp', 'ctx'))
- norm2_gain_grad: float32 [768], P(('fsdp', 'ctx'))
- norm2_bias_grad: float32 [768], P(('fsdp', 'ctx'))
The draws below stay inside these ranges and needn't reach their ends.
Inputs may be any that keep to these rules, and one draw needn't show every extreme that they name: The lengths of each sequence sum to 512, and the longest document of every sequence has exactly 320 tokens.
All inputs are finite; a program needn't handle non-finite values.
Results may differ from the reference program's by a relative error of at most 0.038.
Values may be sent and summed in bfloat16 or wider, within the bound.
No kernel may reach another device: no remote copies, remote signals or barrier semaphores. Data moves between devices by JAX's collectives and lax.ppermute only.
A program may use at most 64 MiB of HBM per device.

```python
import math
import jax
import jax.numpy as jnp
import numpy as np
from jax import lax

D = 768
H = 12
HD = 64
FF = 3072
DOCS = 6
SEQS = 4
LEN = 512


def draw_tokens(key, part):
    whole_shape = (SEQS, LEN, D)
    result = jnp.clip(jax.random.normal(key, whole_shape, jnp.float32), -10.0, 10.0)
    return result.astype(jnp.bfloat16)


def draw_qkv_weight(key, part):
    result = jnp.clip(jax.random.normal(key, (3, D, D), jnp.float32) * D ** (-0.5), -0.25, 0.25)
    return result.astype(jnp.bfloat16)


def with_spikes(drawn, key, source, target, parts, factor):
    def block_of(axis_at):
        return (jnp.arange(drawn.shape[axis_at]) // (drawn.shape[axis_at] // parts)).reshape((-1,) + (1,) * (drawn.ndim - 1 - axis_at))

    one_side = jax.random.permutation(key, parts)[block_of(target)]
    second = (block_of(target) + parts // 2) % parts
    return jnp.where((block_of(source) == one_side) | (block_of(source) == second), factor * drawn, drawn)


def levels(rng, dims, pieces, low, high):
    level = 1.0
    for dim, parts in pieces:
        heights = jax.random.uniform(jax.random.fold_in(jax.random.fold_in(rng, 6), dim), (parts,), jnp.float32, low / len(pieces), high / len(pieces))
        level = level * jnp.repeat(jnp.exp(heights), dims[dim] // parts).reshape((-1,) + (1,) * (len(dims) - 1 - dim))
    return level


def split_up(amount, total, reach, skew):
    loads = [(1 << 20) // math.isqrt(grade ** skew) + 1 for grade in range(2, amount + 1)]
    spare, holding = total - reach - (amount - 1), [1] * (amount - 1)
    while spare > 0:
        movable = [i for i in range(amount - 1) if holding[i] < reach]
        mass, left = sum([loads[i] for i in movable]), spare
        for i in movable:
            addition = min(reach - holding[i], max(1, left * loads[i] // mass), spare)
            holding[i] = holding[i] + addition
            spare = spare - addition
    return np.array([reach] + holding)


def uneven_parts(stream_key, amount, total, limit, skew):
    if amount == 2:
        one = jax.random.randint(stream_key, (), max(1, total - limit), min(limit, total - 1) + 1)
        return jnp.stack([one, total - one])
    tallies = jnp.asarray(split_up(amount, total, limit, skew), jnp.int32)
    pairs = (amount - 1) // 2
    source_of, taker = tallies[1:1 + 2 * pairs:2], tallies[2:2 + 2 * pairs:2]
    slack = jnp.minimum(source_of - 1, limit - taker)
    shifted = jax.random.randint(jax.random.fold_in(stream_key, 1), (pairs,), 0, 1 << 20) % (slack + 1)
    tallies = tallies.at[1:1 + 2 * pairs:2].set(source_of - shifted).at[2:2 + 2 * pairs:2].set(taker + shifted)
    return tallies[jax.random.permutation(jax.random.fold_in(stream_key, 2), amount)]


def noise(rng, shape, scale, bound, cuts=(), kind=jnp.bfloat16):
    loudness = levels(rng, shape, cuts, -0.22, 0.18) if cuts else 1.0
    entries = jax.random.normal(rng, shape, jnp.float32) * scale * loudness
    return jnp.minimum(jnp.maximum(entries, -bound), bound).astype(kind)


def bell_draw_with(stream_key, dims, spread, bound, shards, heavy, kind=jnp.bfloat16):
    values = spread * jax.random.normal(stream_key, dims, jnp.float32)
    if shards:
        values = values * levels(stream_key, dims, shards, -0.22, 0.18)
    return jnp.clip(with_spikes(values, jax.random.fold_in(stream_key, 3), *heavy), -bound, bound).astype(kind)


def setup_inputs(seed: int = 0) -> dict:
    key_list = jax.random.split(jax.random.key(seed), 16)
    return {
        "tokens": draw_tokens(jax.random.fold_in(key_list[15], 71), 0),
        "lengths": jax.vmap(lambda own: uneven_parts(own, DOCS, LEN, 5 * LEN // 8, 2))(jax.random.split(key_list[1], SEQS)).reshape((SEQS, DOCS)).astype(jnp.int32),
        "qkv_weight": draw_qkv_weight(jax.random.fold_in(key_list[15], 71), 0),
        "qv_bias": noise(key_list[3], (2, H, HD), 0.5, 3.0, ((1, 4), (2, 8))),
        "out_weight": noise(key_list[4], (D, D), (D // 16) ** -0.5, 0.875, ((0, 4), (1, 8))),
        "out_bias": noise(key_list[5], (D,), 0.5, 3.0, ((0, 8),)),
        "norm1_gain": jnp.clip(1.0 + 0.18 * jax.random.normal(key_list[6], (D,), jnp.float32), 0.099609375, 1.8984375).astype(jnp.bfloat16),
        "norm1_bias": noise(key_list[7], (D,), 0.5, 3.0, ((0, 8),)),
        "up_weight": noise(key_list[8], (D, FF), D ** -0.5, 0.21875, ((0, 8), (1, 4))),
        "up_bias": noise(key_list[9], (FF // HD, HD), 0.5, 3.0, ((0, 4), (1, 8))),
        "down_weight": noise(key_list[10], (FF, D), FF ** -0.5, 0.109375, ((0, 4), (1, 8))),
        "down_bias": noise(key_list[11], (D,), 0.5, 3.0, ((0, 8),)),
        "norm2_gain": jnp.clip(1.0 + 0.18 * jax.random.normal(key_list[12], (D,), jnp.float32), 0.099609375, 1.8984375).astype(jnp.bfloat16),
        "norm2_bias": noise(key_list[13], (D,), 0.5, 3.0, ((0, 8),)),
        "cotangent": bell_draw_with(key_list[14], (SEQS, LEN, D), 1.0, 6.0, ((0, 2), (1, 4)), (1, 2, 4, 2.0)),
    }


EPSILON = 1e-12

def doc_labels(seq_lengths):
    doc_ends = jnp.cumsum(seq_lengths).astype(jnp.int32)
    positions = jnp.arange(LEN, dtype=jnp.int32)
    return lax.optimization_barrier(jnp.sum((doc_ends[None, :] <= positions[:, None]).astype(jnp.int32), axis=1)).astype(jnp.int32)

def norm_rows(hidden):
    center = hidden - lax.optimization_barrier(jnp.mean(hidden, axis=-1, keepdims=True))
    inverse = lax.rsqrt(lax.optimization_barrier(jnp.mean(center * center, axis=-1, keepdims=True)) + EPSILON)
    return (center * inverse, inverse)

def norm_back(grad_norm, normed, inverse):
    first_mean = lax.optimization_barrier(jnp.mean(grad_norm, axis=-1, keepdims=True))
    second_mean = lax.optimization_barrier(jnp.mean(grad_norm * normed, axis=-1, keepdims=True))
    return inverse * (grad_norm - first_mean - normed * second_mean)

def gelu_parts(pre_act):
    cdf_part = 0.5 * (1.0 + lax.erf(pre_act * (1.0 / math.sqrt(2.0))))
    density = jnp.exp(-0.5 * pre_act * pre_act) * (1.0 / math.sqrt(2.0 * math.pi))
    return (pre_act * cdf_part, cdf_part + pre_act * density)

def masked_scores(queries, key_rows, same_doc):
    scores = jnp.dot(queries, key_rows.T, preferred_element_type=jnp.float32) * (1.0 / math.sqrt(HD))
    return jnp.where(same_doc, scores, -jnp.inf)

def head_forward(inputs, same_doc):
    queries, key_rows, value_rows = inputs
    scores = masked_scores(queries, key_rows, same_doc)
    row_max = lax.optimization_barrier(jnp.max(scores, axis=1, keepdims=True))
    log_total = row_max + jnp.log(lax.optimization_barrier(jnp.sum(jnp.exp(scores - row_max), axis=1, keepdims=True)))
    probs = jnp.exp(scores - log_total).astype(jnp.bfloat16)
    head_out = jnp.dot(probs, value_rows, preferred_element_type=jnp.float32).astype(jnp.bfloat16)
    return (head_out, log_total[:, 0])

def head_backward(inputs, same_doc):
    queries, key_rows, value_rows, head_out, grad_out, log_total = inputs
    scores = masked_scores(queries, key_rows, same_doc)
    probs = jnp.exp(scores - log_total[:, None])
    delta = lax.optimization_barrier(jnp.sum(grad_out.astype(jnp.float32) * head_out.astype(jnp.float32), axis=1, keepdims=True))
    grad_probs = jnp.dot(grad_out, value_rows.T, preferred_element_type=jnp.float32)
    grad_scores = (probs * (grad_probs - delta)).astype(jnp.bfloat16)
    score_scale = 1.0 / math.sqrt(HD)
    grad_query = jnp.dot(grad_scores, key_rows, preferred_element_type=jnp.float32) * score_scale
    grad_key = jnp.dot(grad_scores.T, queries, preferred_element_type=jnp.float32) * score_scale
    grad_value = jnp.dot(probs.astype(jnp.bfloat16).T, grad_out, preferred_element_type=jnp.float32)
    return (grad_query, grad_key, grad_value)

def split_heads(rows):
    return rows.reshape(LEN, H, HD).transpose(1, 0, 2)

def join_heads(heads):
    return heads.transpose(1, 0, 2).reshape(LEN, D)

def one_sequence(seq_tokens, seq_lengths, seq_cot, params):
    w_qkv, b_qv, w_out, b_out, gain_one, shift_one, w_up, b_up, w_down, b_down, gain_two, shift_two = params
    labels = doc_labels(seq_lengths)
    same_doc = labels[:, None] == labels[None, :]
    queries = (jnp.dot(seq_tokens, w_qkv[0], preferred_element_type=jnp.float32) + b_qv[0].reshape(D)).astype(jnp.bfloat16)
    key_rows = jnp.dot(seq_tokens, w_qkv[1], preferred_element_type=jnp.float32).astype(jnp.bfloat16)
    value_rows = (jnp.dot(seq_tokens, w_qkv[2], preferred_element_type=jnp.float32) + b_qv[1].reshape(D)).astype(jnp.bfloat16)
    query_heads = split_heads(queries)
    key_heads = split_heads(key_rows)
    value_heads = split_heads(value_rows)

    def forward_head(inputs):
        return head_forward(inputs, same_doc)
    head_out, log_total = lax.map(forward_head, (query_heads, key_heads, value_heads))
    attended = join_heads(head_out)
    residual_one = seq_tokens.astype(jnp.float32) + (jnp.dot(attended, w_out, preferred_element_type=jnp.float32) + b_out)
    normed_one, inverse_one = norm_rows(residual_one)
    middle = normed_one * gain_one + shift_one
    middle_b = middle.astype(jnp.bfloat16)
    pre_act = jnp.dot(middle_b, w_up, preferred_element_type=jnp.float32) + b_up.reshape(FF)
    activated, gelu_slope = gelu_parts(pre_act)
    activated_b = activated.astype(jnp.bfloat16)
    residual_two = middle + (jnp.dot(activated_b, w_down, preferred_element_type=jnp.float32) + b_down)
    normed_two, inverse_two = norm_rows(residual_two)
    output = (normed_two * gain_two + shift_two).astype(jnp.bfloat16)
    grad_in = seq_cot.astype(jnp.float32)
    d_gain_two = lax.optimization_barrier(jnp.sum(grad_in * normed_two, axis=0))
    d_shift_two = lax.optimization_barrier(jnp.sum(grad_in, axis=0))
    d_res_two = norm_back(grad_in * gain_two, normed_two, inverse_two)
    d_down_bias = lax.optimization_barrier(jnp.sum(d_res_two, axis=0))
    d_res_two_b = d_res_two.astype(jnp.bfloat16)
    d_down = jnp.dot(activated_b.T, d_res_two_b, preferred_element_type=jnp.float32)
    d_pre = jnp.dot(d_res_two_b, w_down.T, preferred_element_type=jnp.float32) * gelu_slope
    d_up_bias = lax.optimization_barrier(jnp.sum(d_pre, axis=0)).reshape(FF // HD, HD)
    d_pre_b = d_pre.astype(jnp.bfloat16)
    d_up = jnp.dot(middle_b.T, d_pre_b, preferred_element_type=jnp.float32)
    d_middle = d_res_two + jnp.dot(d_pre_b, w_up.T, preferred_element_type=jnp.float32)
    d_gain_one = lax.optimization_barrier(jnp.sum(d_middle * normed_one, axis=0))
    d_shift_one = lax.optimization_barrier(jnp.sum(d_middle, axis=0))
    d_res_one = norm_back(d_middle * gain_one, normed_one, inverse_one)
    d_out_bias = lax.optimization_barrier(jnp.sum(d_res_one, axis=0))
    d_res_one_b = d_res_one.astype(jnp.bfloat16)
    d_out = jnp.dot(attended.T, d_res_one_b, preferred_element_type=jnp.float32)
    d_attended = jnp.dot(d_res_one_b, w_out.T, preferred_element_type=jnp.float32).astype(jnp.bfloat16)

    def backward_head(inputs):
        return head_backward(inputs, same_doc)
    grad_q, grad_k, grad_v = lax.map(backward_head, (query_heads, key_heads, value_heads, head_out, split_heads(d_attended), log_total))
    d_query = join_heads(grad_q)
    d_key = join_heads(grad_k)
    d_value = join_heads(grad_v)
    d_qv_bias = jnp.stack([lax.optimization_barrier(jnp.sum(d_query, axis=0)), lax.optimization_barrier(jnp.sum(d_value, axis=0))]).reshape(2, H, HD)
    query_b = d_query.astype(jnp.bfloat16)
    key_b = d_key.astype(jnp.bfloat16)
    value_b = d_value.astype(jnp.bfloat16)
    d_qkv = jnp.stack([jnp.dot(seq_tokens.T, query_b, preferred_element_type=jnp.float32), jnp.dot(seq_tokens.T, key_b, preferred_element_type=jnp.float32), jnp.dot(seq_tokens.T, value_b, preferred_element_type=jnp.float32)])
    back_sum = jnp.dot(query_b, w_qkv[0].T, preferred_element_type=jnp.float32)
    back_sum = back_sum + jnp.dot(key_b, w_qkv[1].T, preferred_element_type=jnp.float32)
    back_sum = back_sum + jnp.dot(value_b, w_qkv[2].T, preferred_element_type=jnp.float32)
    token_grad = (d_res_one + back_sum).astype(jnp.bfloat16)
    grads = (d_qkv, d_qv_bias, d_out, d_out_bias, d_gain_one, d_shift_one, d_up, d_up_bias, d_down, d_down_bias, d_gain_two, d_shift_two)
    return ((output, token_grad), grads)

def reference(tokens, lengths, qkv_weight, qv_bias, out_weight, out_bias, norm1_gain, norm1_bias, up_weight, up_bias, down_weight, down_bias, norm2_gain, norm2_bias, cotangent):
    params = (qkv_weight, qv_bias, out_weight, out_bias, norm1_gain, norm1_bias, up_weight, up_bias, down_weight, down_bias, norm2_gain, norm2_bias)

    def accumulate(totals, sequence):
        seq_tokens, seq_lengths, seq_cot = sequence
        results, grads = one_sequence(seq_tokens, seq_lengths, seq_cot, params)
        return (jax.tree.map(jnp.add, totals, grads), results)
    initial = (jnp.zeros((3, D, D), jnp.float32), jnp.zeros((2, H, HD), jnp.float32), jnp.zeros((D, D), jnp.float32), jnp.zeros((D,), jnp.float32), jnp.zeros((D,), jnp.float32), jnp.zeros((D,), jnp.float32), jnp.zeros((D, FF), jnp.float32), jnp.zeros((FF // HD, HD), jnp.float32), jnp.zeros((FF, D), jnp.float32), jnp.zeros((D,), jnp.float32), jnp.zeros((D,), jnp.float32), jnp.zeros((D,), jnp.float32))
    totals, results = lax.scan(accumulate, initial, (tokens, lengths, cotangent))
    outputs, token_grads = results
    return (outputs, token_grads, totals[0], totals[1], totals[2], totals[3], totals[4], totals[5], totals[6], totals[7], totals[8], totals[9], totals[10], totals[11])
```

```python
import math

import jax
import jax.numpy as jnp
from jax import lax
from jax.sharding import PartitionSpec as P

EPSILON = 1e-12
BF = jnp.bfloat16
F32 = jnp.float32


def norm_rows(hidden):
    center = hidden - jnp.mean(hidden, axis=-1, keepdims=True)
    inverse = lax.rsqrt(jnp.mean(center * center, axis=-1, keepdims=True) + EPSILON)
    return (center * inverse, inverse)


def norm_back(grad_norm, normed, inverse):
    first_mean = jnp.mean(grad_norm, axis=-1, keepdims=True)
    second_mean = jnp.mean(grad_norm * normed, axis=-1, keepdims=True)
    return inverse * (grad_norm - first_mean - normed * second_mean)


def gelu_parts(pre_act):
    cdf_part = 0.5 * (1.0 + lax.erf(pre_act * (1.0 / math.sqrt(2.0))))
    density = jnp.exp(-0.5 * pre_act * pre_act) * (1.0 / math.sqrt(2.0 * math.pi))
    return (pre_act * cdf_part, cdf_part + pre_act * density)


def dot(left, right, dims):
    return lax.dot_general(left, right, ((dims[0], dims[1]), ((), ())), preferred_element_type=F32)


def ring(value, axis, step):
    size = lax.axis_size(axis)
    return lax.ppermute(value, axis, [(i, (i + step) % size) for i in range(size)])


def flip(value, axis, bit):
    size = lax.axis_size(axis)
    return lax.ppermute(value, axis, [(i, i ^ bit) for i in range(size)])


def near_first(size):
    return sorted(range(1, size), key=lambda k: min(k, size - k))


def gather_blocks(shard):
    rows_of, cols_of = lax.axis_size("fsdp"), lax.axis_size("ctx")
    if rows_of > 2:
        return lax.all_gather(shard, ("fsdp", "ctx"), axis=0)
    row, col = lax.axis_index("fsdp"), lax.axis_index("ctx")
    whole = jnp.zeros((rows_of * cols_of,) + shard.shape, shard.dtype)
    for step in [0] + near_first(cols_of):
        block = ring(shard, "ctx", step) if step else shard
        source = (col - step) % cols_of
        whole = lax.dynamic_update_index_in_dim(whole, block, row * cols_of + source, 0)
        for other in range(1, rows_of):
            moved = ring(block, "fsdp", other)
            place = ((row - other) % rows_of) * cols_of + source
            whole = lax.dynamic_update_index_in_dim(whole, moved, place, 0)
    return whole


def scatter_blocks(parts):
    rows_of, cols_of = lax.axis_size("fsdp"), lax.axis_size("ctx")
    row, col = lax.axis_index("fsdp"), lax.axis_index("ctx")
    if rows_of > 2:
        return lax.psum_scatter(parts.astype(F32), ("fsdp", "ctx"), scatter_dimension=0)
    parts = parts.reshape((rows_of, cols_of) + parts.shape[1:])
    kept = lax.dynamic_index_in_dim(parts, row, 0, False)
    for other in range(1, rows_of):
        gone = lax.dynamic_index_in_dim(parts, (row + other) % rows_of, 0, False)
        kept = (kept.astype(F32) + ring(gone, "fsdp", other).astype(F32)).astype(BF)
    return scatter_ctx(kept)


def scatter_ctx(kept):
    cols_of, col = lax.axis_size("ctx"), lax.axis_index("ctx")
    total = lax.dynamic_index_in_dim(kept, col, 0, False).astype(F32)
    for step in near_first(cols_of):
        gone = lax.dynamic_index_in_dim(kept, (col + step) % cols_of, 0, False)
        total = total + ring(gone, "ctx", step).astype(F32)
    return total


def gather_rows(rows):
    cols_of, col = lax.axis_size("ctx"), lax.axis_index("ctx")
    lanes_of, lane = lax.axis_size("tp"), lax.axis_index("tp")
    share = rows.shape[0] // lanes_of
    own = lax.dynamic_slice_in_dim(rows, lane * share, share, 0)
    order = near_first(cols_of)
    held = jnp.stack([ring(own, "ctx", step) for step in order])[None]
    masks = [0]
    bit = lanes_of // 2
    while bit:
        held = jnp.concatenate([held, flip(held, "tp", bit)], axis=0)
        masks = masks + [mask ^ bit for mask in masks]
        bit //= 2
    whole = jnp.zeros((cols_of, lanes_of, share) + rows.shape[1:], rows.dtype)
    whole = lax.dynamic_update_index_in_dim(whole, rows.reshape(whole.shape[1:]), col, 0)
    for at, step in enumerate(order):
        for which, mask in enumerate(masks):
            start = ((col - step) % cols_of, lane ^ mask, 0, 0)
            whole = lax.dynamic_update_slice(whole, held[which, at][None, None], start)
    return whole.reshape((cols_of,) + rows.shape)


def half_of(value, which):
    size = value.shape[0] // 2
    return lax.dynamic_slice_in_dim(value, which * size, size, 0)


def sum_half(part):
    parity = lax.axis_index("tp") & 1
    total = half_of(part, parity).astype(F32)
    total = total + flip(half_of(part, 1 - parity), "tp", 1).astype(F32)
    bit = 2
    while bit < lax.axis_size("tp"):
        sent = total.astype(BF)
        total = sent.astype(F32) + flip(sent, "tp", bit).astype(F32)
        bit *= 2
    return total


def join_halves(half):
    parity = lax.axis_index("tp") & 1
    other = flip(half, "tp", 1)
    first = jnp.where(parity == 0, half, other)
    second = jnp.where(parity == 0, other, half)
    return jnp.concatenate([first, second], axis=0)


def body(
    tokens,
    lengths,
    qkv_weight,
    qv_bias,
    out_weight,
    out_bias,
    norm1_gain,
    norm1_bias,
    up_weight,
    up_bias,
    down_weight,
    down_bias,
    norm2_gain,
    norm2_bias,
    cotangent,
):
    seq_count, local_len, width = tokens.shape
    cols_of, col = lax.axis_size("ctx"), lax.axis_index("ctx")
    blocks = lax.axis_size("fsdp") * cols_of
    place = lax.axis_index("fsdp") * cols_of + col
    parity = lax.axis_index("tp") & 1
    shard = width // blocks
    local_heads = qv_bias.shape[1]
    piece = qv_bias.shape[2]
    head_size = piece * blocks
    inner = local_heads * head_size
    hidden = up_weight.shape[1]
    scale = 1.0 / math.sqrt(head_size)
    total_len = local_len * cols_of
    rows = tokens.reshape(-1, width)

    vectors = jnp.stack([out_bias, norm1_gain, norm1_bias, down_bias, norm2_gain, norm2_bias])
    vectors = lax.dynamic_update_slice(jnp.zeros((6, width), BF), vectors, (0, place * shard))
    up_row = lax.dynamic_update_slice(
        jnp.zeros((up_bias.shape[0], head_size), BF), up_bias, (0, place * piece)
    ).reshape(1, hidden)
    qv_row = lax.dynamic_update_slice(
        jnp.zeros((2, local_heads, head_size), BF), qv_bias, (0, 0, place * piece)
    ).reshape(1, 2 * inner)
    qv_row = jnp.pad(qv_row, ((0, 0), (0, width - 2 * inner)))
    small = jnp.concatenate([vectors, up_row, qv_row, jnp.zeros((8, width), BF)], axis=0)
    first_pack = jnp.concatenate(
        [
            jnp.concatenate([qkv_weight[0], qkv_weight[1], qkv_weight[2], out_weight.T], axis=1),
            small,
        ],
        axis=0,
    )
    second_pack = jnp.concatenate([up_weight, down_weight.T], axis=0)
    all_rows = gather_rows(rows)
    first_all = gather_blocks(first_pack)
    second_all = gather_blocks(second_pack)
    mixed = first_all[:, :shard].reshape(width, 4 * inner)
    w_q, w_k, w_v, w_out_t = (mixed[:, i * inner : (i + 1) * inner] for i in range(4))
    small_all = jnp.sum(first_all[:, shard:].astype(F32), axis=0)
    b_out, gain_one, shift_one, b_down, gain_two, shift_two = (small_all[i] for i in range(6))
    b_up = small_all[6]
    b_q, b_v = small_all[7, :inner], small_all[7, inner : 2 * inner]
    w_up = second_all[:, :shard].reshape(width, hidden)
    w_down_t = second_all[:, shard:].reshape(width, hidden)

    doc_ends = jnp.cumsum(lengths, axis=1)
    key_at = jnp.arange(total_len, dtype=jnp.int32)
    labels = jnp.sum((doc_ends[:, None, :] <= key_at[None, :, None]).astype(jnp.int32), axis=2)
    own_labels = lax.dynamic_slice_in_dim(labels, col * local_len, local_len, 1)
    same = (own_labels[:, :, None] == labels[:, None, :])[:, None]

    def by_head(flat):
        return flat.reshape(seq_count, -1, local_heads, head_size).transpose(0, 2, 1, 3)

    def all_keys(flat):
        flat = flat.reshape(cols_of, seq_count, local_len, local_heads, head_size)
        return flat.transpose(1, 3, 0, 2, 4).reshape(
            seq_count, local_heads, total_len, head_size
        )

    flat_rows = all_rows.reshape(-1, width)
    queries = by_head((dot(rows, w_q, ((1,), (0,))) + b_q).astype(BF))
    key_rows = all_keys(dot(flat_rows, w_k, ((1,), (0,))).astype(BF))
    value_rows = all_keys((dot(flat_rows, w_v, ((1,), (0,))) + b_v).astype(BF))
    scores = jnp.einsum("shqd,shkd->shqk", queries, key_rows, preferred_element_type=F32) * scale
    scores = jnp.where(same, scores, -jnp.inf)
    weights = jnp.exp(scores - jnp.max(scores, axis=3, keepdims=True))
    probs = weights / jnp.sum(weights, axis=3, keepdims=True)
    probs_b = probs.astype(BF)
    attended = jnp.einsum("shqk,shkd->shqd", probs_b, value_rows, preferred_element_type=F32)
    attended = attended.transpose(0, 2, 1, 3).reshape(-1, inner).astype(BF)
    attn_part = dot(attended, w_out_t, ((1,), (1,))).astype(BF)

    residual_one = half_of(rows, parity).astype(F32) + sum_half(attn_part) + b_out
    normed_one, inverse_one = norm_rows(residual_one)
    middle = normed_one * gain_one + shift_one
    middle_b = join_halves(middle.astype(BF))
    pre_act = dot(middle_b, w_up, ((1,), (0,))) + b_up
    activated, slope = gelu_parts(pre_act)
    activated_b = activated.astype(BF)
    down_part = dot(activated_b, w_down_t, ((1,), (1,))).astype(BF)
    residual_two = middle + sum_half(down_part) + b_down
    normed_two, inverse_two = norm_rows(residual_two)
    output = (normed_two * gain_two + shift_two).astype(BF)

    grad_in = half_of(cotangent.reshape(-1, width), parity).astype(F32)
    d_gain_two = jnp.sum(grad_in * normed_two, axis=0)
    d_shift_two = jnp.sum(grad_in, axis=0)
    d_res_two = norm_back(grad_in * gain_two, normed_two, inverse_two)
    d_down_bias = jnp.sum(d_res_two, axis=0)
    d_res_two_b = join_halves(d_res_two.astype(BF))
    d_pre = dot(d_res_two_b, w_down_t, ((1,), (0,))) * slope
    d_up_bias = jnp.sum(d_pre, axis=0)
    d_pre_b = d_pre.astype(BF)
    up_back = dot(d_pre_b, w_up, ((1,), (1,))).astype(BF)
    d_up = dot(middle_b, d_pre_b, ((0,), (0,))).astype(BF)
    d_down_t = dot(d_res_two_b, activated_b, ((0,), (0,))).astype(BF)
    second_grads = scatter_blocks(
        jnp.concatenate(
            [d_up.reshape(blocks, shard, hidden), d_down_t.reshape(blocks, shard, hidden)], axis=1
        )
    )
    d_middle = d_res_two + sum_half(up_back)
    d_gain_one = jnp.sum(d_middle * normed_one, axis=0)
    d_shift_one = jnp.sum(d_middle, axis=0)
    d_res_one = norm_back(d_middle * gain_one, normed_one, inverse_one)
    d_out_bias = jnp.sum(d_res_one, axis=0)
    d_res_one_b = join_halves(d_res_one.astype(BF))
    d_out_t = dot(d_res_one_b, attended, ((0,), (0,)))
    d_heads_flat = dot(d_res_one_b, w_out_t, ((1,), (0,))).astype(BF)
    d_heads = by_head(d_heads_flat)
    delta = jnp.sum(d_heads.astype(F32) * by_head(attended).astype(F32), axis=3)
    grad_probs = jnp.einsum("shqd,shkd->shqk", d_heads, value_rows, preferred_element_type=F32)
    grad_scores = (probs * (grad_probs - delta[..., None])).astype(BF)
    d_query = (
        jnp.einsum("shqk,shkd->sqhd", grad_scores, key_rows, preferred_element_type=F32) * scale
    ).reshape(-1, inner)
    d_key = (
        jnp.einsum("shqk,shqd->skhd", grad_scores, queries, preferred_element_type=F32) * scale
    ).reshape(seq_count, cols_of, local_len, inner)
    d_value = jnp.einsum("shqk,shqd->skhd", probs_b, d_heads, preferred_element_type=F32).reshape(
        seq_count, cols_of, local_len, inner
    )
    query_b = d_query.astype(BF)
    key_value = (
        jnp.concatenate([d_key, d_value], axis=3)
        .astype(BF)
        .transpose(1, 0, 2, 3)
        .reshape(cols_of, -1, 2 * inner)
    )
    own_kv = scatter_ctx(key_value).astype(BF)
    back_part = dot(query_b, w_q, ((1,), (1,)))
    back_part = back_part + dot(own_kv[:, :inner], w_k, ((1,), (1,)))
    back_part = back_part + dot(own_kv[:, inner:], w_v, ((1,), (1,)))
    token_grad = join_halves((d_res_one + sum_half(back_part.astype(BF))).astype(BF))

    d_w_q = dot(rows, query_b, ((0,), (0,)))
    d_w_kv = dot(flat_rows, key_value.reshape(-1, 2 * inner), ((0,), (0,)))
    d_mixed = jnp.concatenate([d_w_q, d_w_kv, d_out_t], axis=1).astype(BF)
    qv_sum = jnp.concatenate([jnp.sum(d_query, axis=0), jnp.sum(d_value, axis=(0, 1, 2))])
    halves = jnp.stack(
        [d_out_bias, d_gain_one, d_shift_one, d_down_bias, d_gain_two, d_shift_two]
    )
    halves = halves + flip(halves, "tp", 1)
    small_grads = jnp.concatenate(
        [
            halves,
            d_up_bias[None],
            jnp.pad(qv_sum, (0, width - 2 * inner))[None],
            jnp.zeros((8, width), F32),
        ],
        axis=0,
    ).astype(BF)
    first_grads = scatter_blocks(
        jnp.concatenate(
            [
                d_mixed.reshape(blocks, shard, 4 * inner),
                jnp.broadcast_to(small_grads[None], (blocks,) + small_grads.shape),
            ],
            axis=1,
        )
    )
    g_mixed, g_small = first_grads[:shard], first_grads[shard:]
    g_qkv = jnp.stack([g_mixed[:, i * inner : (i + 1) * inner] for i in range(3)])
    g_out = g_mixed[:, 3 * inner :].T
    g_vectors = lax.dynamic_slice(g_small, (0, place * shard), (6, shard))
    g_up_bias = lax.dynamic_slice(
        g_small[6].reshape(up_bias.shape[0], head_size), (0, place * piece), up_bias.shape
    )
    g_qv = lax.dynamic_slice(
        g_small[7, : 2 * inner].reshape(2, local_heads, head_size),
        (0, 0, place * piece),
        qv_bias.shape,
    )
    return (
        join_halves(output).reshape(tokens.shape),
        token_grad.reshape(tokens.shape),
        g_qkv,
        g_qv,
        g_out,
        g_vectors[0],
        g_vectors[1],
        g_vectors[2],
        second_grads[:shard],
        g_up_bias,
        second_grads[shard:].T,
        g_vectors[3],
        g_vectors[4],
        g_vectors[5],
    )


def solution(mesh):
    split = ("fsdp", "ctx")
    vector = P(split)
    rows = P("fsdp", "ctx", None)
    weights = (
        P(None, split, "tp"),
        P(None, "tp", split),
        P("tp", split),
        vector,
        vector,
        vector,
        P(split, "tp"),
        P("tp", split),
        P("tp", split),
        vector,
        vector,
        vector,
    )
    return jax.shard_map(
        body,
        mesh=mesh,
        in_specs=(rows, P("fsdp", None)) + weights + (rows,),
        out_specs=(rows, rows) + weights,
        check_vma=False,
    )
```

```python
import functools
import math

import jax
import jax.numpy as jnp
from jax import lax
from jax.experimental import pallas as pl
from jax.experimental.pallas import tpu as pltpu
from jax.sharding import PartitionSpec as P


EPSILON = 1e-12
BF = jnp.bfloat16
F32 = jnp.float32
TAIL = 8


def norm_rows(hidden):
    center = hidden - jnp.mean(hidden, axis=-1, keepdims=True)
    inverse = lax.rsqrt(jnp.mean(center * center, axis=-1, keepdims=True) + EPSILON)
    return (center * inverse, inverse)


def norm_back(grad_norm, normed, inverse):
    first_mean = jnp.mean(grad_norm, axis=-1, keepdims=True)
    second_mean = jnp.mean(grad_norm * normed, axis=-1, keepdims=True)
    return inverse * (grad_norm - first_mean - normed * second_mean)


def gelu_parts(pre_act):
    cdf_part = 0.5 * (1.0 + lax.erf(pre_act * (1.0 / math.sqrt(2.0))))
    density = jnp.exp(-0.5 * pre_act * pre_act) * (1.0 / math.sqrt(2.0 * math.pi))
    return (pre_act * cdf_part, cdf_part + pre_act * density)


def dot(left, right, over_left, over_right):
    return lax.dot_general(
        left, right, (((over_left,), (over_right,)), ((), ())), preferred_element_type=F32
    )


def ring(value, axis, step):
    size = lax.axis_size(axis)
    return lax.ppermute(value, axis, [(i, (i + step) % size) for i in range(size)])


def flip(value, axis, bit):
    size = lax.axis_size(axis)
    return lax.ppermute(value, axis, [(i, i ^ bit) for i in range(size)])


def near_first(size):
    return sorted(range(1, size), key=lambda k: min(k, size - k))


def call(kernel, outs, args, smem=(), scratch=(), flops=0):
    size = sum(math.prod(s) * jnp.dtype(t).itemsize for s, t in outs)
    size += sum(a.size * a.dtype.itemsize for a in args)
    vmem = pl.BlockSpec(memory_space=pltpu.VMEM)
    table = pl.BlockSpec(memory_space=pltpu.SMEM)
    return pallas(kernel, outs, args, smem, scratch, flops, size, vmem, table)


def pallas(kernel, outs, args, smem, scratch, flops, size, vmem, table):
    return pl.pallas_call(
        kernel,
        out_shape=tuple(jax.ShapeDtypeStruct(s, t) for s, t in outs),
        in_specs=[table] * len(smem) + [vmem] * len(args),
        out_specs=tuple(vmem for _ in outs),
        scratch_shapes=list(scratch),
        cost_estimate=pl.CostEstimate(flops=flops, bytes_accessed=size, transcendentals=0),
    )(*smem, *args)


def lanes(low, high, width):
    at = lax.broadcasted_iota(jnp.int32, (1, width), 1)
    return (at >= low) & (at < high)


def aligned(start, size):
    return pl.ds(pl.multiple_of(start, size), size)


class Sizes:
    def __init__(self, tokens, qv_bias, up_weight):
        self.seqs, self.local, self.width = tokens.shape
        self.rows = self.seqs * self.local
        self.fsdp, self.ctx, self.tp = (lax.axis_size(a) for a in ("fsdp", "ctx", "tp"))
        self.blocks = self.fsdp * self.ctx
        self.shard = self.width // self.blocks
        self.heads, self.piece = qv_bias.shape[1:]
        self.head = self.piece * self.blocks
        self.inner = self.heads * self.head
        self.pair = 2 * self.inner
        self.hidden = up_weight.shape[1]
        self.total = self.local * self.ctx
        self.half = self.rows // 2
        self.scale = 1.0 / math.sqrt(self.head)
        self.direct = self.fsdp == 2 and self.shard % 16 == 0


def attention_kernel(z, order, masks, *refs):
    (meta, lengths), refs = refs[:2], refs[2:]
    count = z.blocks if z.direct else 1
    blocks, refs = refs[:count], refs[count:]
    own, refs = refs[0], refs[1:]
    pieces, refs = refs[: len(masks)], refs[len(masks) :]
    mixed, small, every, keys, query, probs, att, kept, sent = refs[:9]
    part = refs[9]
    row, col, lane = meta[0], meta[1], meta[2]
    if z.direct:
        places = block_places(z, order, row, col)
        total = jnp.zeros((TAIL, z.width), F32)
        for block, place in zip(blocks, places):
            mixed[aligned(place * z.shard, z.shard), :] = block[: z.shard, :]
            total = total + block[z.shard :, :].astype(F32)
        small[...] = total
    else:
        mixed[...] = blocks[0][: z.width, :]
        small[...] = blocks[0][z.width :, :].astype(F32)
    every[col] = own[...]
    share = z.rows // z.tp
    for at, step in enumerate(order):
        source = lax.rem(col - step + z.ctx, z.ctx)
        for which, mask in enumerate(masks):
            spot = jnp.bitwise_xor(lane, mask) * share
            every[source, aligned(spot, share), :] = pieces[which][at]
    b_q = jnp.where(lanes(0, z.inner, z.pair), small[7:8, : z.pair], 0.0)
    b_kv = jnp.where(lanes(z.inner, z.pair, z.pair), small[7:8, : z.pair], 0.0)

    @pl.loop(0, z.ctx)
    def _(at):
        both = dot(every[at], mixed[:, z.pair :], 1, 0) + b_kv
        both = both.astype(BF)
        for seq in range(z.seqs):
            piece = both[seq * z.local : (seq + 1) * z.local]
            keys[seq, aligned(at * z.local, z.local), :] = piece

    flat = dot(own[...], mixed[:, : z.pair], 1, 0) + b_q
    query[...] = jnp.where(lanes(0, z.inner, z.pair), flat, 0.0).astype(BF)
    docs = lengths.shape[1]
    key_at = lax.broadcasted_iota(jnp.int32, (1, z.total), 1)
    query_at = lax.broadcasted_iota(jnp.int32, (z.local, 1), 0) + col * z.local
    for seq in range(z.seqs):
        key_label = jnp.zeros((1, z.total), jnp.int32)
        query_label = jnp.zeros((z.local, 1), jnp.int32)
        end = 0
        for doc in range(docs):
            end = end + lengths[seq, doc]
            key_label = key_label + jnp.where(key_at >= end, 1, 0)
            query_label = query_label + jnp.where(query_at >= end, 1, 0)
        same = query_label == key_label
        flat = query[seq * z.local : (seq + 1) * z.local, :]
        result = jnp.zeros((z.local, z.pair), F32)
        for head in range(z.heads):
            low = head * z.head
            chosen = jnp.where(lanes(low, low + z.head, z.pair), flat, jnp.zeros_like(flat))
            scores = dot(chosen, keys[seq], 1, 1) * z.scale
            scores = jnp.where(same, scores, -1e30)
            weights = jnp.exp(scores - jnp.max(scores, axis=1, keepdims=True))
            chance = weights * (1.0 / jnp.sum(weights, axis=1, keepdims=True))
            chance = chance.astype(BF)
            probs[seq * z.heads + head] = chance
            low = low + z.inner
            found = dot(chance, keys[seq], 1, 0)
            result = jnp.where(lanes(low, low + z.head, z.pair), found, result)
        att[seq * z.local : (seq + 1) * z.local, :] = result.astype(BF)
    part[...] = dot(att[...], mixed[:, : z.pair], 1, 1)
    split_halves(z, lane, part, kept, sent)


def block_places(z, order, row, col):
    places = []
    for step in [0] + order:
        source = lax.rem(col - step + z.ctx, z.ctx)
        places.append(row * z.ctx + source)
        places.append((1 - row) * z.ctx + source)
    return places


def split_halves(z, lane, part, kept, sent):
    parity = jnp.bitwise_and(lane, 1)
    kept[...] = part[aligned(parity * z.half, z.half), :]
    sent[...] = part[aligned((1 - parity) * z.half, z.half), :].astype(sent.dtype)


def place_halves(z, lane, own, other, whole):
    parity = jnp.bitwise_and(lane, 1)
    whole[aligned(parity * z.half, z.half), :] = own[...].astype(F32)
    whole[aligned((1 - parity) * z.half, z.half), :] = other[...].astype(F32)


def forward_kernel(z, order, *refs):
    meta, own, other, rows, small = refs[:5]
    count = z.blocks if z.direct else 1
    blocks, refs = refs[5 : 5 + count], refs[5 + count :]
    up, down, normed_one, inverse_one, middle_b, slope, active, kept, sent = refs[:9]
    work = refs[9]
    row, col, lane = meta[0], meta[1], meta[2]
    if z.direct:
        for block, place in zip(blocks, block_places(z, order, row, col)):
            up[aligned(place * z.shard, z.shard), :] = block[: z.shard, :]
            down[aligned(place * z.shard, z.shard), :] = block[z.shard :, :]
    else:
        up[...] = blocks[0][: z.width, :]
        down[...] = blocks[0][z.width :, :]
    place_halves(z, lane, own, other, work)
    hidden = rows[...].astype(F32) + work[...] + small[0:1, :]
    normed, inverse = norm_rows(hidden)
    normed_one[...] = normed
    inverse_one[...] = inverse
    middle_b[...] = (normed * small[1:2, :] + small[2:3, :]).astype(BF)
    pre = dot(middle_b[...], up[...], 1, 0) + small[6:7, :]
    activated, gradient = gelu_parts(pre)
    slope[...] = gradient
    active[...] = activated.astype(BF)
    work[...] = dot(active[...], down[...], 1, 1)
    split_halves(z, lane, work, kept, sent)


def middle_kernel(z, *refs):
    meta, own, other, normed_one, small, cotangent, up, down, slope = refs[:9]
    output, d_two, d_two_b, d_pre_b, kept, sent, sums, work = refs[9:]
    lane = meta[2]
    place_halves(z, lane, own, other, work)
    middle = normed_one[...] * small[1:2, :] + small[2:3, :]
    normed, inverse = norm_rows(middle + work[...] + small[3:4, :])
    output[...] = (normed * small[4:5, :] + small[5:6, :]).astype(BF)
    grad_in = cotangent[...].astype(F32)
    sums[...] = jnp.zeros_like(sums)
    sums[4:5, :] = jnp.sum(grad_in * normed, axis=0, keepdims=True)
    sums[5:6, :] = jnp.sum(grad_in, axis=0, keepdims=True)
    d_res = norm_back(grad_in * small[4:5, :], normed, inverse)
    sums[3:4, :] = jnp.sum(d_res, axis=0, keepdims=True)
    d_two[...] = d_res
    d_two_b[...] = d_res.astype(BF)
    d_pre = dot(d_two_b[...], down[...], 1, 0) * slope[...]
    sums[6:7, :] = jnp.sum(d_pre, axis=0, keepdims=True)
    d_pre_b[...] = d_pre.astype(BF)
    work[...] = dot(d_pre_b[...], up[...], 1, 1)
    split_halves(z, lane, work, kept, sent)


def second_grad_kernel(z, *refs):
    meta, middle_b, d_pre_b, d_two_b, active = refs[:5]
    kept, sent, work = refs[5:]
    pairs = ((middle_b, d_pre_b), (d_two_b, active))
    for at, (left, right) in enumerate(pairs):
        work[...] = dot(left[...], right[...], 0, 0).astype(BF)
        part = z.width // 2
        kept[at] = work[aligned(meta[0] * part, part), :]
        sent[at] = work[aligned((1 - meta[0]) * part, part), :]


def second_grad_whole_kernel(*refs):
    _, middle_b, d_pre_b, d_two_b, active, out = refs
    out[0] = dot(middle_b[...], d_pre_b[...], 0, 0).astype(BF)
    out[1] = dot(d_two_b[...], active[...], 0, 0).astype(BF)


def backward_kernel(z, order, *refs):
    (meta, own, other, d_two, normed_one, inverse_one, small, mixed, att, query, keys), refs = (
        refs[:11],
        refs[11:],
    )
    (probs, sums_in), refs = refs[:2], refs[2:]
    d_one, d_one_b, d_query, d_keys, sums = refs[:5]
    sends, refs = refs[5 : 4 + z.ctx], refs[4 + z.ctx :]
    work, grads = refs
    col, lane = meta[1], meta[2]
    place_halves(z, lane, own, other, work)
    d_middle = d_two[...] + work[...]
    normed = normed_one[...]
    sums[...] = sums_in[...]
    sums[1:2, :] = jnp.sum(d_middle * normed, axis=0, keepdims=True)
    sums[2:3, :] = jnp.sum(d_middle, axis=0, keepdims=True)
    d_res = norm_back(d_middle * small[1:2, :], normed, inverse_one[...])
    sums[0:1, :] = jnp.sum(d_res, axis=0, keepdims=True)
    d_one[...] = d_res
    d_one_b[...] = d_res.astype(BF)
    upper = lanes(z.inner, z.pair, z.pair)
    d_att = jnp.where(upper, dot(d_one_b[...], mixed[:, : z.pair], 1, 0), 0.0).astype(BF)
    qv_sum = jnp.zeros((1, z.pair), F32)
    for seq in range(z.seqs):
        span = slice(seq * z.local, (seq + 1) * z.local)
        d_here, a_here, q_here = d_att[span], att[span, :], query[span, :]
        product = d_here.astype(F32) * a_here.astype(F32)
        d_q = jnp.zeros((z.local, z.pair), F32)
        for head in range(z.heads):
            low = head * z.head
            near = lanes(low, low + z.head, z.pair)
            far = lanes(low + z.inner, low + z.inner + z.head, z.pair)
            q_head = jnp.where(near, q_here, jnp.zeros_like(q_here))
            d_head = jnp.where(far, d_here, jnp.zeros_like(d_here))
            delta = jnp.sum(jnp.where(far, product, 0.0), axis=1, keepdims=True)
            chance = probs[seq * z.heads + head]
            d_chance = dot(d_head, keys[seq], 1, 1)
            d_scores = (chance.astype(F32) * (d_chance - delta)).astype(BF)
            d_q = jnp.where(near, dot(d_scores, keys[seq], 1, 0), d_q)
            d_kv = dot(d_scores, q_head, 0, 0) * z.scale + dot(chance, d_head, 0, 0)
            if head == 0:
                grads[...] = d_kv
            else:
                grads[...] += d_kv
        d_q = d_q * z.scale
        qv_sum = qv_sum + jnp.sum(d_q, axis=0, keepdims=True)
        qv_sum = qv_sum + jnp.where(upper, jnp.sum(grads[...], axis=0, keepdims=True), 0.0)
        d_query[span, :] = d_q.astype(BF)
        for at in range(z.ctx):
            d_keys[at, span, :] = grads[at * z.local : (at + 1) * z.local, :].astype(BF)
    sums[7:8, : z.pair] = qv_sum
    for step, send in zip(order, sends):
        send[...] = d_keys[lax.rem(col + step, z.ctx)]


def first_grad_kernel(z, *refs):
    meta, rows, every, d_query, d_keys, d_one_b, att, sums = refs[:8]
    outs, work = refs[8:-1], refs[-1]
    near = dot(rows[...], d_query[...], 0, 0) + dot(d_one_b[...], att[...], 0, 0)
    work[:, : z.pair] = near.astype(BF)
    far = dot(every[0], d_keys[0], 0, 0)
    for at in range(1, z.ctx):
        far = far + dot(every[at], d_keys[at], 0, 0)
    work[:, z.pair :] = far.astype(BF)
    if len(outs) == 1:
        outs[0][...] = work[...]
        return
    part = z.width // 2
    for out, start in zip(outs, (meta[0] * part, (1 - meta[0]) * part)):
        out[:part, :] = work[aligned(start, part), :]
        out[part:, :] = sums[...].astype(BF)


def back_kernel(z, *refs):
    meta, d_keys, d_query, mixed = refs[:4]
    got, refs = refs[4 : 3 + z.ctx], refs[3 + z.ctx :]
    kept, sent, work = refs
    total = d_keys[meta[1]].astype(F32)
    for piece in got:
        total = total + piece[...].astype(F32)
    work[...] = dot(d_query[...], mixed[:, : z.pair], 1, 1)
    work[...] += dot(total.astype(BF), mixed[:, z.pair :], 1, 1)
    split_halves(z, meta[2], work, kept, sent)


def token_kernel(z, meta, own, other, d_one, out, work):
    place_halves(z, meta[2], own, other, work)
    out[...] = (d_one[...] + work[...]).astype(BF)


def where_equal(shape, left, right):
    rows = lax.broadcasted_iota(jnp.int32, shape, 0)
    cols = lax.broadcasted_iota(jnp.int32, shape, 1)
    return jnp.where(left(rows) == right(cols), 1.0, 0.0).astype(BF)


def same_head(z, heads, width):
    rows = lax.broadcasted_iota(jnp.int32, (heads, width), 0)
    cols = lax.broadcasted_iota(jnp.int32, (heads, width), 1)
    return (cols >= rows * z.head) & (cols < (rows + 1) * z.head)


def qv_lanes(z, head):
    start = lax.broadcasted_iota(jnp.int32, (2, z.width), 0) * z.inner + head * z.head
    cols = lax.broadcasted_iota(jnp.int32, (2, z.width), 1)
    return (cols >= start) & (cols < start + z.head)


def pack_kernel(z, *refs):
    meta, qkv, out, up_bias, qv_bias, rows = refs[:6]
    vectors, (pack, share) = refs[6:-2], refs[-2:]
    place = meta[0] * z.ctx + meta[1]
    inner = z.inner

    def spread(at):
        return where_equal((inner, z.width), lambda r: r + at * inner, lambda c: c)

    total = dot(qkv[0], spread(0), 1, 0) + dot(out[...], spread(1), 0, 0)
    total = total + dot(qkv[1], spread(2), 1, 0) + dot(qkv[2], spread(3), 1, 0)
    pack[: z.shard, :] = total.astype(BF)
    at = place * z.shard
    chosen = where_equal((z.shard, z.width), lambda r: r + at, lambda c: c)
    lines = [dot(vector[...], chosen, 1, 0) for vector in vectors]
    at = place * z.piece
    chosen = where_equal(
        (z.piece, z.width), lambda r: r + at, lambda c: jnp.bitwise_and(c, z.head - 1)
    )
    heads = up_bias.shape[1]
    wide = jnp.where(same_head(z, heads, z.width), dot(up_bias[...], chosen, 0, 0), 0.0)
    lines.append(jnp.sum(wide, axis=0, keepdims=True))
    line = jnp.zeros((1, z.width), F32)
    for head in range(z.heads):
        wide = jnp.where(qv_lanes(z, head), dot(qv_bias[head], chosen, 1, 0), 0.0)
        line = line + jnp.sum(wide, axis=0, keepdims=True)
    lines.append(line)
    pack[z.shard :, :] = jnp.concatenate(lines, axis=0).astype(BF)
    size = z.rows // z.tp
    share[...] = rows[aligned(meta[2] * size, size), :]


def pack_plain(z, place, qkv_weight, out_weight, vectors, up_bias, qv_bias):
    vectors = lax.dynamic_update_slice(jnp.zeros((6, z.width), BF), vectors, (0, place * z.shard))
    up_row = lax.dynamic_update_slice(
        jnp.zeros((up_bias.shape[0], z.head), BF), up_bias, (0, place * z.piece)
    ).reshape(1, z.hidden)
    qv_row = lax.dynamic_update_slice(
        jnp.zeros((2, z.heads, z.head), BF), qv_bias, (0, 0, place * z.piece)
    ).reshape(1, z.pair)
    qv_row = jnp.pad(qv_row, ((0, 0), (0, z.width - z.pair)))
    tail = jnp.concatenate([vectors, up_row, qv_row], axis=0)
    mixed = jnp.concatenate([qkv_weight[0], out_weight.T, qkv_weight[1], qkv_weight[2]], axis=1)
    return mixed, tail


def terms(value):
    high = value.astype(BF)
    rest = value - high.astype(F32)
    middle = rest.astype(BF)
    return high, middle, (rest - middle.astype(F32)).astype(BF)


def exact_dot(left, right, over_left, over_right):
    if left.dtype == F32:
        return sum(dot(term, right, over_left, over_right) for term in terms(left))
    return sum(dot(left, term, over_left, over_right) for term in terms(right))


def finish_first_kernel(z, meta, *refs):
    blocks, refs = refs[: z.ctx], refs[z.ctx :]
    (g_qkv, g_out, g_up_bias, g_qv), g_vectors = refs[:4], refs[4:]
    total = blocks[0][...].astype(F32)
    for block in blocks[1:]:
        total = total + block[...].astype(F32)
    inner = z.inner
    for at, start in enumerate((0, 2 * inner, 3 * inner)):
        g_qkv[at] = total[: z.shard, start : start + inner]
    eye = where_equal((z.shard, z.shard), lambda r: r, lambda c: c)
    g_out[...] = exact_dot(total[: z.shard, inner : 2 * inner], eye, 0, 0)
    small = total[z.shard :]
    place = meta[0] * z.ctx + meta[1]
    at = place * z.shard
    chosen = where_equal((z.width, z.shard), lambda r: r, lambda c: c + at)
    for line, vector in enumerate(g_vectors):
        vector[...] = exact_dot(small[line : line + 1], chosen, 1, 0)
    at = place * z.piece
    chosen = where_equal(
        (z.width, z.piece), lambda r: jnp.bitwise_and(r, z.head - 1), lambda c: c + at
    )
    heads = g_up_bias.shape[1]
    wide = jnp.where(same_head(z, heads, z.width), small[6:7], 0.0)
    g_up_bias[...] = exact_dot(chosen, wide, 0, 1)
    for head in range(z.heads):
        wide = jnp.where(qv_lanes(z, head), small[7:8], 0.0)
        g_qv[head] = exact_dot(wide, chosen, 1, 0)


def finish_second_kernel(z, *refs):
    blocks, (g_up, g_down_t) = refs[: z.ctx], refs[z.ctx :]
    up, down = blocks[0][0].astype(F32), blocks[0][1].astype(F32)
    for block in blocks[1:]:
        up = up + block[0].astype(F32)
        down = down + block[1].astype(F32)
    g_up[...] = up
    g_down_t[...] = down


def share_kernel(z, order, *refs):
    meta, kept, got = refs[:3]
    own, sends, work = refs[3], refs[4:-1], refs[-1]
    work[...] = (kept[...].astype(F32) + got[...].astype(F32)).astype(BF)
    for step, out in zip([0] + order, (own,) + tuple(sends)):
        start = lax.rem(meta[1] + step, z.ctx) * z.shard
        if len(work.shape) == 3:
            for at in range(work.shape[0]):
                out[at] = work[at, aligned(start, z.shard), :]
        else:
            out[: z.shard, :] = work[aligned(start, z.shard), :]
            out[z.shard :, :] = work[z.ctx * z.shard :, :]


def gather_blocks(order, shard):
    found = []
    for step in [0] + order:
        block = ring(shard, "ctx", step) if step else shard
        found += [block, ring(block, "fsdp", 1)]
    return found


def sum_rows(z, kept, sent):
    total = kept + flip(sent, "tp", 1).astype(F32)
    bit = 2
    while bit < z.tp:
        mine = total.astype(BF)
        total = mine.astype(F32) + flip(mine, "tp", bit).astype(F32)
        bit *= 2
    total = total.astype(BF)
    return total, flip(total, "tp", 1)


def reduce_shared(z, order, meta, kept, sent):
    got = ring(sent, "fsdp", 1)
    shape = kept.shape[:-2] + (kept.shape[-2] - (z.ctx - 1) * z.shard, kept.shape[-1])
    if len(shape) == 3:
        shape = (shape[0], z.shard, shape[2])
    pieces = call(
        functools.partial(share_kernel, z, order),
        [(shape, BF)] * z.ctx,
        (kept, got),
        smem=(meta,),
        scratch=[pltpu.VMEM(kept.shape, BF)],
    )
    got = [ring(piece, "ctx", step) for step, piece in zip(order, pieces[1:])]
    return [pieces[0]] + got


def body(
    tokens,
    lengths,
    qkv_weight,
    qv_bias,
    out_weight,
    out_bias,
    norm1_gain,
    norm1_bias,
    up_weight,
    up_bias,
    down_weight,
    down_bias,
    norm2_gain,
    norm2_bias,
    cotangent,
):
    z = Sizes(tokens, qv_bias, up_weight)
    rows = tokens.reshape(-1, z.width)
    row, col, lane = (lax.axis_index(a).astype(jnp.int32) for a in ("fsdp", "ctx", "tp"))
    meta = jnp.stack([row, col, lane])
    place = row * z.ctx + col
    order = near_first(z.ctx)
    full = (z.rows, z.width)
    half = (z.half, z.width)
    square = (z.width, z.width)

    vectors = (out_bias, norm1_gain, norm1_bias, down_bias, norm2_gain, norm2_bias)
    if z.direct:
        first_pack, token_share = call(
            functools.partial(pack_kernel, z),
            [((z.shard + TAIL, z.width), BF), ((z.rows // z.tp, z.width), BF)],
            (
                qkv_weight,
                out_weight,
                up_bias.T,
                qv_bias.transpose(1, 0, 2),
                rows,
                *(vector.reshape(1, z.shard) for vector in vectors),
            ),
            smem=(meta,),
        )
    else:
        mixed_shard, tail = pack_plain(
            z, place, qkv_weight, out_weight, jnp.stack(vectors), up_bias, qv_bias
        )
        share = z.rows // z.tp
        token_share = lax.dynamic_slice_in_dim(rows, lane * share, share, 0)
    got = jnp.stack([ring(token_share, "ctx", step) for step in order])
    pieces, masks = [got], [0]
    bit = z.tp // 2
    while bit:
        pieces = pieces + [flip(piece, "tp", bit) for piece in pieces]
        masks = masks + [mask ^ bit for mask in masks]
        bit //= 2
    second_pack = jnp.concatenate([up_weight, down_weight.T], axis=0)
    if z.direct:
        first_blocks = gather_blocks(order, first_pack)
        second_blocks = gather_blocks(order, second_pack)
    else:
        split = ("fsdp", "ctx")
        mixed_all = lax.all_gather(mixed_shard, split, axis=0, tiled=True)
        tail_all = jnp.sum(lax.all_gather(tail, split, axis=0).astype(F32), axis=0).astype(BF)
        first_blocks = [jnp.concatenate([mixed_all, tail_all], axis=0)]
        second_all = lax.all_gather(second_pack, split, axis=0)
        second_all = second_all.reshape(z.blocks, 2, z.shard, z.hidden).transpose(1, 0, 2, 3)
        second_blocks = [second_all.reshape(2 * z.width, z.hidden)]

    mixed, small, every, keys, query, probs, att, kept, sent = call(
        functools.partial(attention_kernel, z, order, masks),
        [
            (square, BF),
            ((TAIL, z.width), F32),
            ((z.ctx,) + full, BF),
            ((z.seqs, z.total, z.pair), BF),
            ((z.rows, z.pair), BF),
            ((z.seqs * z.heads, z.local, z.total), BF),
            ((z.rows, z.pair), BF),
            (half, F32),
            (half, BF),
        ],
        (*first_blocks, rows, *pieces),
        smem=(meta, lengths),
        scratch=[pltpu.VMEM(full, F32)],
        flops=4 * z.rows * z.ctx * z.width * z.pair,
    )
    own, other = sum_rows(z, kept, sent)
    up, down, normed_one, inverse_one, middle_b, slope, active, kept, sent = call(
        functools.partial(forward_kernel, z, order),
        [
            (square, BF),
            (square, BF),
            (full, F32),
            ((z.rows, 1), F32),
            (full, BF),
            (full, F32),
            (full, BF),
            (half, F32),
            (half, BF),
        ],
        (own, other, rows, small, *second_blocks),
        smem=(meta,),
        scratch=[pltpu.VMEM(full, F32)],
        flops=4 * z.rows * z.width * z.hidden,
    )
    own, other = sum_rows(z, kept, sent)
    output, d_two, d_two_b, d_pre_b, kept, sent, sums = call(
        functools.partial(middle_kernel, z),
        [
            (full, BF),
            (full, F32),
            (full, BF),
            (full, BF),
            (half, F32),
            (half, BF),
            ((TAIL, z.width), F32),
        ],
        (own, other, normed_one, small, cotangent.reshape(full), up, down, slope),
        smem=(meta,),
        scratch=[pltpu.VMEM(full, F32)],
        flops=4 * z.rows * z.width * z.hidden,
    )
    grad_args = (middle_b, d_pre_b, d_two_b, active)
    grad_flops = 4 * z.rows * z.width * z.hidden
    if z.direct:
        part = (2, z.width // 2, z.hidden)
        kept_two, sent_two = call(
            functools.partial(second_grad_kernel, z),
            [(part, BF), (part, BF)],
            grad_args,
            smem=(meta,),
            scratch=[pltpu.VMEM(square, BF)],
            flops=grad_flops,
        )
    else:
        (second_grads,) = call(
            second_grad_whole_kernel,
            [((2,) + square, BF)],
            grad_args,
            smem=(meta,),
            flops=grad_flops,
        )
    own, other = sum_rows(z, kept, sent)
    d_one, d_one_b, d_query, d_keys, sums, *sends = call(
        functools.partial(backward_kernel, z, order),
        [
            (full, F32),
            (full, BF),
            ((z.rows, z.pair), BF),
            ((z.ctx, z.rows, z.pair), BF),
            ((TAIL, z.width), F32),
        ]
        + [((z.rows, z.pair), BF)] * (z.ctx - 1),
        (own, other, d_two, normed_one, inverse_one, small, mixed, att, query, keys, probs, sums),
        smem=(meta,),
        scratch=[pltpu.VMEM(full, F32), pltpu.VMEM((z.total, z.pair), F32)],
        flops=10 * z.rows * z.heads * z.total * z.pair,
    )
    got = [ring(piece, "ctx", step) for step, piece in zip(order, sends)]
    if z.direct:
        part = (z.width // 2 + TAIL, z.width)
        grad_outs = [(part, BF), (part, BF)]
    else:
        grad_outs = [(square, BF)]
    first_parts = call(
        functools.partial(first_grad_kernel, z),
        grad_outs,
        (rows, every, d_query, d_keys, d_one_b, att, sums),
        smem=(meta,),
        scratch=[pltpu.VMEM(square, BF)],
        flops=2 * z.rows * (z.ctx + 2) * z.width * z.pair,
    )
    kept, sent = call(
        functools.partial(back_kernel, z),
        [(half, F32), (half, BF)],
        (d_keys, d_query, mixed, *got),
        smem=(meta,),
        scratch=[pltpu.VMEM(full, F32)],
        flops=4 * z.rows * z.width * z.pair,
    )
    own, other = sum_rows(z, kept, sent)
    (token_grad,) = call(
        functools.partial(token_kernel, z),
        [(full, BF)],
        (own, other, d_one),
        smem=(meta,),
        scratch=[pltpu.VMEM(full, F32)],
    )

    if z.direct:
        second = reduce_shared(z, order, meta, kept_two, sent_two)
        first = reduce_shared(z, order, meta, *first_parts)
        g_up, g_down_t = call(
            functools.partial(finish_second_kernel, z),
            [(up_weight.shape, F32), (up_weight.shape, F32)],
            second,
        )
        g_down = g_down_t.T
        g_qkv, g_out, g_up_bias, g_qv, *g_vectors = call(
            functools.partial(finish_first_kernel, z),
            [
                (qkv_weight.shape, F32),
                (out_weight.shape, F32),
                (up_bias.shape[::-1], F32),
                ((z.heads, 2, z.piece), F32),
            ]
            + [((1, z.shard), F32)] * 6,
            first,
            smem=(meta,),
        )
        g_up_bias = g_up_bias.T
        g_qv = g_qv.transpose(1, 0, 2)
        g_vectors = [vector.reshape(z.shard) for vector in g_vectors]
    else:
        split = ("fsdp", "ctx")
        second = lax.psum_scatter(
            second_grads.astype(F32), split, scatter_dimension=1, tiled=True
        )
        g_up, g_down = second[0], second[1].T
        g_mixed = lax.psum_scatter(
            first_parts[0].astype(F32), split, scatter_dimension=0, tiled=True
        )
        g_small = lax.psum(sums, split)
        inner = z.inner
        starts = (0, 2 * inner, 3 * inner)
        g_qkv = jnp.stack([g_mixed[:, start : start + inner] for start in starts])
        g_out = g_mixed[:, inner : 2 * inner].T
        g_vectors = lax.dynamic_slice(g_small, (0, place * z.shard), (6, z.shard))
        g_up_bias = lax.dynamic_slice(
            g_small[6].reshape(up_bias.shape[0], z.head), (0, place * z.piece), up_bias.shape
        )
        g_qv = lax.dynamic_slice(
            g_small[7, : z.pair].reshape(2, z.heads, z.head),
            (0, 0, place * z.piece),
            qv_bias.shape,
        )
    return (
        output.reshape(tokens.shape),
        token_grad.reshape(tokens.shape),
        g_qkv,
        g_qv,
        g_out,
        g_vectors[0],
        g_vectors[1],
        g_vectors[2],
        g_up,
        g_up_bias,
        g_down,
        g_vectors[3],
        g_vectors[4],
        g_vectors[5],
    )


def solution(mesh):
    split = ("fsdp", "ctx")
    vector = P(split)
    rows = P("fsdp", "ctx", None)
    weights = (
        P(None, split, "tp"),
        P(None, "tp", split),
        P("tp", split),
        vector,
        vector,
        vector,
        P(split, "tp"),
        P("tp", split),
        P("tp", split),
        vector,
        vector,
        vector,
    )

    return jax.shard_map(
        body,
        mesh=mesh,
        in_specs=(rows, P("fsdp", None)) + weights + (rows,),
        out_specs=(rows, rows) + weights,
        check_vma=False,
    )
```

```python
import functools
import math

import jax
import jax.numpy as jnp
from jax import lax
from jax.experimental import pallas as pl
from jax.experimental.pallas import tpu as pltpu
from jax.sharding import PartitionSpec as P


EPSILON = 1e-12
BF = jnp.bfloat16
F32 = jnp.float32
TAIL = 8
SPARE = 8 << 20


def norm_rows(hidden):
    center = hidden - jnp.mean(hidden, axis=-1, keepdims=True)
    inverse = lax.rsqrt(jnp.mean(center * center, axis=-1, keepdims=True) + EPSILON)
    return (center * inverse, inverse)


def norm_back(grad_norm, normed, inverse):
    first_mean = jnp.mean(grad_norm, axis=-1, keepdims=True)
    second_mean = jnp.mean(grad_norm * normed, axis=-1, keepdims=True)
    return inverse * (grad_norm - first_mean - normed * second_mean)


def gelu_parts(pre_act):
    cdf_part = 0.5 * (1.0 + lax.erf(pre_act * (1.0 / math.sqrt(2.0))))
    density = jnp.exp(-0.5 * pre_act * pre_act) * (1.0 / math.sqrt(2.0 * math.pi))
    return (pre_act * cdf_part, cdf_part + pre_act * density)


def dot(left, right, over_left, over_right):
    return lax.dot_general(
        left, right, (((over_left,), (over_right,)), ((), ())), preferred_element_type=F32
    )


def ring(value, axis, step):
    size = lax.axis_size(axis)
    return lax.ppermute(value, axis, [(i, (i + step) % size) for i in range(size)])


def flip(value, axis, bit):
    size = lax.axis_size(axis)
    return lax.ppermute(value, axis, [(i, i ^ bit) for i in range(size)])


def near_first(size):
    return sorted(range(1, size), key=lambda k: min(k, size - k))


def call(kernel, outs, args, smem=(), scratch=(), flops=0, spare=SPARE):
    size = sum(math.prod(s) * jnp.dtype(t).itemsize for s, t in outs)
    size += sum(a.size * a.dtype.itemsize for a in args)
    vmem = pl.BlockSpec(memory_space=pltpu.VMEM)
    table = pl.BlockSpec(memory_space=pltpu.SMEM)
    return pallas(kernel, outs, args, smem, scratch, flops, size, vmem, table, spare)


def pallas(kernel, outs, args, smem, scratch, flops, size, vmem, table, spare):
    held = sum(math.prod(s.shape) * jnp.dtype(s.dtype).itemsize for s in scratch)
    room = size + held + spare
    return pl.pallas_call(
        kernel,
        out_shape=tuple(jax.ShapeDtypeStruct(s, t) for s, t in outs),
        in_specs=[table] * len(smem) + [vmem] * len(args),
        out_specs=tuple(vmem for _ in outs),
        scratch_shapes=list(scratch),
        compiler_params=pltpu.CompilerParams(vmem_limit_bytes=room),
        cost_estimate=pl.CostEstimate(flops=flops, bytes_accessed=size, transcendentals=0),
    )(*smem, *args)


def lanes(low, high, width):
    at = lax.broadcasted_iota(jnp.int32, (1, width), 1)
    return (at >= low) & (at < high)


def aligned(start, size):
    return pl.ds(pl.multiple_of(start, size), size)


class Sizes:
    def __init__(self, tokens, qv_bias, up_weight):
        self.seqs, self.local, self.width = tokens.shape
        self.rows = self.seqs * self.local
        self.fsdp, self.ctx, self.tp = (lax.axis_size(a) for a in ("fsdp", "ctx", "tp"))
        self.blocks = self.fsdp * self.ctx
        self.shard = self.width // self.blocks
        self.heads, self.piece = qv_bias.shape[1:]
        self.head = self.piece * self.blocks
        self.inner = self.heads * self.head
        self.pair = 2 * self.inner
        self.hidden = up_weight.shape[1]
        self.total = self.local * self.ctx
        self.half = self.rows // 2
        self.scale = 1.0 / math.sqrt(self.head)
        self.direct = self.fsdp == 2 and self.shard % 16 == 0


def attention_kernel(z, order, masks, *refs):
    (meta, lengths), refs = refs[:2], refs[2:]
    count = z.blocks if z.direct else 1
    blocks, refs = refs[:count], refs[count:]
    own, refs = refs[0], refs[1:]
    pieces, refs = refs[: len(masks)], refs[len(masks) :]
    mixed, small, every, keys, query, probs, att, kept, sent = refs[:9]
    part = refs[9]
    row, col, lane = meta[0], meta[1], meta[2]
    if z.direct:
        places = block_places(z, order, row, col)
        total = jnp.zeros((TAIL, z.width), F32)
        for block, place in zip(blocks, places):
            mixed[aligned(place * z.shard, z.shard), :] = block[: z.shard, :]
            total = total + block[z.shard :, :].astype(F32)
        small[...] = total
    else:
        mixed[...] = blocks[0][: z.width, :]
        small[...] = blocks[0][z.width :, :].astype(F32)
    every[col] = own[...]
    share = z.rows // z.tp
    for at, step in enumerate(order):
        source = lax.rem(col - step + z.ctx, z.ctx)
        for which, mask in enumerate(masks):
            spot = jnp.bitwise_xor(lane, mask) * share
            every[source, aligned(spot, share), :] = pieces[which][at]
    b_q = jnp.where(lanes(0, z.inner, z.pair), small[7:8, : z.pair], 0.0)
    b_kv = jnp.where(lanes(z.inner, z.pair, z.pair), small[7:8, : z.pair], 0.0)

    @pl.loop(0, z.ctx)
    def _(at):
        both = dot(every[at], mixed[:, z.pair :], 1, 0) + b_kv
        both = both.astype(BF)
        for seq in range(z.seqs):
            piece = both[seq * z.local : (seq + 1) * z.local]
            keys[seq, aligned(at * z.local, z.local), :] = piece

    flat = dot(own[...], mixed[:, : z.pair], 1, 0) + b_q
    query[...] = jnp.where(lanes(0, z.inner, z.pair), flat, 0.0).astype(BF)
    docs = lengths.shape[1]
    key_at = lax.broadcasted_iota(jnp.int32, (1, z.total), 1)
    query_at = lax.broadcasted_iota(jnp.int32, (z.local, 1), 0) + col * z.local
    for seq in range(z.seqs):
        key_label = jnp.zeros((1, z.total), jnp.int32)
        query_label = jnp.zeros((z.local, 1), jnp.int32)
        end = 0
        for doc in range(docs):
            end = end + lengths[seq, doc]
            key_label = key_label + jnp.where(key_at >= end, 1, 0)
            query_label = query_label + jnp.where(query_at >= end, 1, 0)
        same = query_label == key_label
        flat = query[seq * z.local : (seq + 1) * z.local, :]
        result = jnp.zeros((z.local, z.pair), F32)
        for head in range(z.heads):
            low = head * z.head
            chosen = jnp.where(lanes(low, low + z.head, z.pair), flat, jnp.zeros_like(flat))
            scores = dot(chosen, keys[seq], 1, 1) * z.scale
            scores = jnp.where(same, scores, -1e30)
            weights = jnp.exp(scores - jnp.max(scores, axis=1, keepdims=True))
            chance = weights * (1.0 / jnp.sum(weights, axis=1, keepdims=True))
            chance = chance.astype(BF)
            probs[seq * z.heads + head] = chance
            low = low + z.inner
            found = dot(chance, keys[seq], 1, 0)
            result = jnp.where(lanes(low, low + z.head, z.pair), found, result)
        att[seq * z.local : (seq + 1) * z.local, :] = result.astype(BF)
    part[...] = dot(att[...], mixed[:, : z.pair], 1, 1)
    split_halves(z, lane, part, kept, sent)


def block_places(z, order, row, col):
    places = []
    for step in [0] + order:
        source = lax.rem(col - step + z.ctx, z.ctx)
        places.append(row * z.ctx + source)
        places.append((1 - row) * z.ctx + source)
    return places


def split_halves(z, lane, part, kept, sent):
    parity = jnp.bitwise_and(lane, 1)
    kept[...] = part[aligned(parity * z.half, z.half), :]
    sent[...] = part[aligned((1 - parity) * z.half, z.half), :].astype(sent.dtype)


def place_halves(z, lane, own, other, whole):
    parity = jnp.bitwise_and(lane, 1)
    whole[aligned(parity * z.half, z.half), :] = own[...].astype(F32)
    whole[aligned((1 - parity) * z.half, z.half), :] = other[...].astype(F32)


def forward_kernel(z, order, *refs):
    meta, own, other, rows, small = refs[:5]
    count = z.blocks if z.direct else 1
    blocks, refs = refs[5 : 5 + count], refs[5 + count :]
    up, down, normed_one, inverse_one, middle_b, slope, active, kept, sent, shown = refs[:10]
    work = refs[10]
    row, col, lane = meta[0], meta[1], meta[2]
    if z.direct:
        for block, place in zip(blocks, block_places(z, order, row, col)):
            up[aligned(place * z.shard, z.shard), :] = block[: z.shard, :]
            down[aligned(place * z.shard, z.shard), :] = block[z.shard :, :]
    else:
        up[...] = blocks[0][: z.width, :]
        down[...] = blocks[0][z.width :, :]
    place_halves(z, lane, own, other, work)
    hidden = rows[...].astype(F32) + work[...] + small[0:1, :]
    normed, inverse = norm_rows(hidden)
    normed_one[...] = normed
    inverse_one[...] = inverse
    middle_b[...] = (normed * small[1:2, :] + small[2:3, :]).astype(BF)
    pre = dot(middle_b[...], up[...], 1, 0) + small[6:7, :]
    activated, gradient = gelu_parts(pre)
    slope[...] = gradient
    active[...] = activated.astype(BF)
    show(z, row, middle_b, active, shown)
    work[...] = dot(active[...], down[...], 1, 1)
    split_halves(z, lane, work, kept, sent)


def show(z, row, columns, whole, shown):
    part = z.width // 2
    shown[:, :part] = half_columns(z, 1 - row, columns)
    shown[:, part:] = whole[...]


def half_columns(z, which, columns):
    part = z.width // 2
    return jnp.where(which == 0, columns[:, :part], columns[:, part:])


def middle_kernel(z, *refs):
    meta, own, other, normed_one, small, cotangent, up, down, slope = refs[:9]
    output, d_two, d_two_b, d_pre_b, kept, sent, sums, shown, work = refs[9:]
    lane = meta[2]
    place_halves(z, lane, own, other, work)
    middle = normed_one[...] * small[1:2, :] + small[2:3, :]
    normed, inverse = norm_rows(middle + work[...] + small[3:4, :])
    output[...] = (normed * small[4:5, :] + small[5:6, :]).astype(BF)
    grad_in = cotangent[...].astype(F32)
    sums[...] = jnp.zeros_like(sums)
    sums[4:5, :] = jnp.sum(grad_in * normed, axis=0, keepdims=True)
    sums[5:6, :] = jnp.sum(grad_in, axis=0, keepdims=True)
    d_res = norm_back(grad_in * small[4:5, :], normed, inverse)
    sums[3:4, :] = jnp.sum(d_res, axis=0, keepdims=True)
    d_two[...] = d_res
    d_two_b[...] = d_res.astype(BF)
    d_pre = dot(d_two_b[...], down[...], 1, 0) * slope[...]
    sums[6:7, :] = jnp.sum(d_pre, axis=0, keepdims=True)
    d_pre_b[...] = d_pre.astype(BF)
    show(z, meta[0], d_two_b, d_pre_b, shown)
    work[...] = dot(d_pre_b[...], up[...], 1, 1)
    split_halves(z, lane, work, kept, sent)


def second_grad_kernel(z, order, *refs):
    meta, middle_b, d_pre_b, d_two_b, active, acts, grads = refs[:7]
    outs, work = refs[7:-1], refs[-1]
    part = z.width // 2
    total = dot(half_columns(z, meta[0], middle_b), d_pre_b[...], 0, 0)
    total = total + dot(acts[:, :part], grads[:, part:], 0, 0)
    work[0] = total.astype(BF)
    total = dot(half_columns(z, meta[0], d_two_b), active[...], 0, 0)
    total = total + dot(grads[:, :part], acts[:, part:], 0, 0)
    work[1] = total.astype(BF)
    for step, out in zip([0] + order, outs):
        start = lax.rem(meta[1] + step, z.ctx) * z.shard
        for at in range(2):
            out[at] = work[at, aligned(start, z.shard), :]


def second_grad_whole_kernel(*refs):
    _, middle_b, d_pre_b, d_two_b, active, out = refs
    out[0] = dot(middle_b[...], d_pre_b[...], 0, 0).astype(BF)
    out[1] = dot(d_two_b[...], active[...], 0, 0).astype(BF)


def backward_kernel(z, *refs):
    (meta, own, other, d_two, normed_one, inverse_one, small, mixed, att, query, keys), refs = (
        refs[:11],
        refs[11:],
    )
    (probs, sums_in), refs = refs[:2], refs[2:]
    d_one, d_one_b, d_query, d_keys, sums, kept, sent = refs[:7]
    work, grads, back = refs[7:]
    col, lane = meta[1], meta[2]
    place_halves(z, lane, own, other, work)
    d_middle = d_two[...] + work[...]
    normed = normed_one[...]
    sums[...] = sums_in[...]
    sums[1:2, :] = jnp.sum(d_middle * normed, axis=0, keepdims=True)
    sums[2:3, :] = jnp.sum(d_middle, axis=0, keepdims=True)
    d_res = norm_back(d_middle * small[1:2, :], normed, inverse_one[...])
    sums[0:1, :] = jnp.sum(d_res, axis=0, keepdims=True)
    d_one[...] = d_res
    d_one_b[...] = d_res.astype(BF)
    upper = lanes(z.inner, z.pair, z.pair)
    d_att = jnp.where(upper, dot(d_one_b[...], mixed[:, : z.pair], 1, 0), 0.0).astype(BF)
    qv_sum = jnp.zeros((1, z.pair), F32)
    for seq in range(z.seqs):
        span = slice(seq * z.local, (seq + 1) * z.local)
        d_here, a_here, q_here = d_att[span], att[span, :], query[span, :]
        product = d_here.astype(F32) * a_here.astype(F32)
        d_q = jnp.zeros((z.local, z.pair), F32)
        for head in range(z.heads):
            low = head * z.head
            near = lanes(low, low + z.head, z.pair)
            far = lanes(low + z.inner, low + z.inner + z.head, z.pair)
            q_head = jnp.where(near, q_here, jnp.zeros_like(q_here))
            d_head = jnp.where(far, d_here, jnp.zeros_like(d_here))
            delta = jnp.sum(jnp.where(far, product, 0.0), axis=1, keepdims=True)
            chance = probs[seq * z.heads + head]
            d_chance = dot(d_head, keys[seq], 1, 1)
            d_scores = (chance.astype(F32) * (d_chance - delta)).astype(BF)
            d_q = jnp.where(near, dot(d_scores, keys[seq], 1, 0), d_q)
            d_kv = dot(d_scores, q_head, 0, 0) * z.scale + dot(chance, d_head, 0, 0)
            if head == 0:
                grads[...] = d_kv
            else:
                grads[...] += d_kv
        d_q = d_q * z.scale
        qv_sum = qv_sum + jnp.sum(d_q, axis=0, keepdims=True)
        qv_sum = qv_sum + jnp.where(upper, jnp.sum(grads[...], axis=0, keepdims=True), 0.0)
        d_query[span, :] = d_q.astype(BF)
        for at in range(z.ctx):
            d_keys[at, span, :] = grads[at * z.local : (at + 1) * z.local, :].astype(BF)
    sums[7:8, : z.pair] = qv_sum
    for at in range(z.ctx):
        back[at] = dot(d_keys[at], mixed[:, z.pair :], 1, 1)
    back[col] += dot(d_query[...], mixed[:, : z.pair], 1, 1)
    parity = jnp.bitwise_and(lane, 1)
    kept[...] = back[:, aligned(parity * z.half, z.half), :]
    sent[...] = back[:, aligned((1 - parity) * z.half, z.half), :].astype(BF)


def first_grad_kernel(z, *refs):
    meta, rows, every, d_query, d_keys, d_one_b, att, sums = refs[:8]
    outs, work = refs[8:-1], refs[-1]
    near = dot(rows[...], d_query[...], 0, 0) + dot(d_one_b[...], att[...], 0, 0)
    work[:, : z.pair] = near.astype(BF)
    far = dot(every[0], d_keys[0], 0, 0)
    for at in range(1, z.ctx):
        far = far + dot(every[at], d_keys[at], 0, 0)
    work[:, z.pair :] = far.astype(BF)
    if len(outs) == 1:
        outs[0][...] = work[...]
        return
    part = z.width // 2
    for out, start in zip(outs, (meta[0] * part, (1 - meta[0]) * part)):
        out[:part, :] = work[aligned(start, part), :]
        out[part:, :] = sums[...].astype(BF)


def cut_kernel(z, meta, kept, got, near, far):
    chip = lax.shift_right_logical(meta[2], 1)
    size = z.half // 2
    for out, which in ((near, chip), (far, 1 - chip)):
        span = aligned(which * size, size)
        out[...] = (kept[:, span, :] + got[:, span, :].astype(F32)).astype(out.dtype)


def spread_kernel(z, order, meta, kept, got, own, *sends):
    for step, out in zip([0] + order, (own,) + sends):
        at = lax.rem(meta[1] + step, z.ctx)
        out[...] = (kept[at] + got[at].astype(F32)).astype(out.dtype)


def token_kernel(z, masks, meta, *refs):
    pieces, (d_one, out) = refs[:-2], refs[-2:]
    size = z.rows // z.tp
    for mask, piece in zip(masks, pieces):
        lane = jnp.bitwise_xor(meta[2], mask)
        start = jnp.bitwise_and(lane, 1) * z.half + lax.shift_right_logical(lane, 1) * size
        span = aligned(start, size)
        out[span, :] = (d_one[span, :] + piece[...].astype(F32)).astype(BF)


def where_equal(shape, left, right):
    rows = lax.broadcasted_iota(jnp.int32, shape, 0)
    cols = lax.broadcasted_iota(jnp.int32, shape, 1)
    return jnp.where(left(rows) == right(cols), 1.0, 0.0).astype(BF)


def same_head(z, heads, width):
    rows = lax.broadcasted_iota(jnp.int32, (heads, width), 0)
    cols = lax.broadcasted_iota(jnp.int32, (heads, width), 1)
    return (cols >= rows * z.head) & (cols < (rows + 1) * z.head)


def qv_lanes(z, head):
    start = lax.broadcasted_iota(jnp.int32, (2, z.width), 0) * z.inner + head * z.head
    cols = lax.broadcasted_iota(jnp.int32, (2, z.width), 1)
    return (cols >= start) & (cols < start + z.head)


def pack_kernel(z, *refs):
    meta, qkv, out, up_bias, qv_bias, rows = refs[:6]
    vectors, (pack, share) = refs[6:-2], refs[-2:]
    place = meta[0] * z.ctx + meta[1]
    inner = z.inner

    def spread(at):
        return where_equal((inner, z.width), lambda r: r + at * inner, lambda c: c)

    total = dot(qkv[0], spread(0), 1, 0) + dot(out[...], spread(1), 0, 0)
    total = total + dot(qkv[1], spread(2), 1, 0) + dot(qkv[2], spread(3), 1, 0)
    pack[: z.shard, :] = total.astype(BF)
    at = place * z.shard
    chosen = where_equal((z.shard, z.width), lambda r: r + at, lambda c: c)
    lines = [dot(vector[...], chosen, 1, 0) for vector in vectors]
    at = place * z.piece
    chosen = where_equal(
        (z.piece, z.width), lambda r: r + at, lambda c: jnp.bitwise_and(c, z.head - 1)
    )
    heads = up_bias.shape[1]
    wide = jnp.where(same_head(z, heads, z.width), dot(up_bias[...], chosen, 0, 0), 0.0)
    lines.append(jnp.sum(wide, axis=0, keepdims=True))
    line = jnp.zeros((1, z.width), F32)
    for head in range(z.heads):
        wide = jnp.where(qv_lanes(z, head), dot(qv_bias[head], chosen, 1, 0), 0.0)
        line = line + jnp.sum(wide, axis=0, keepdims=True)
    lines.append(line)
    pack[z.shard :, :] = jnp.concatenate(lines, axis=0).astype(BF)
    size = z.rows // z.tp
    share[...] = rows[aligned(meta[2] * size, size), :]


def pack_plain(z, place, qkv_weight, out_weight, vectors, up_bias, qv_bias):
    vectors = lax.dynamic_update_slice(jnp.zeros((6, z.width), BF), vectors, (0, place * z.shard))
    up_row = lax.dynamic_update_slice(
        jnp.zeros((up_bias.shape[0], z.head), BF), up_bias, (0, place * z.piece)
    ).reshape(1, z.hidden)
    qv_row = lax.dynamic_update_slice(
        jnp.zeros((2, z.heads, z.head), BF), qv_bias, (0, 0, place * z.piece)
    ).reshape(1, z.pair)
    qv_row = jnp.pad(qv_row, ((0, 0), (0, z.width - z.pair)))
    tail = jnp.concatenate([vectors, up_row, qv_row], axis=0)
    mixed = jnp.concatenate([qkv_weight[0], out_weight.T, qkv_weight[1], qkv_weight[2]], axis=1)
    return mixed, tail


def terms(value):
    high = value.astype(BF)
    rest = value - high.astype(F32)
    middle = rest.astype(BF)
    return high, middle, (rest - middle.astype(F32)).astype(BF)


def exact_dot(left, right, over_left, over_right):
    if left.dtype == F32:
        return sum(dot(term, right, over_left, over_right) for term in terms(left))
    return sum(dot(left, term, over_left, over_right) for term in terms(right))


def finish_first_kernel(z, meta, *refs):
    blocks, refs = refs[: z.ctx], refs[z.ctx :]
    (g_qkv, g_out, g_up_bias, g_qv), g_vectors = refs[:4], refs[4:]
    total = blocks[0][...].astype(F32)
    for block in blocks[1:]:
        total = total + block[...].astype(F32)
    inner = z.inner
    for at, start in enumerate((0, 2 * inner, 3 * inner)):
        g_qkv[at] = total[: z.shard, start : start + inner]
    eye = where_equal((z.shard, z.shard), lambda r: r, lambda c: c)
    g_out[...] = exact_dot(total[: z.shard, inner : 2 * inner], eye, 0, 0)
    small = total[z.shard :]
    place = meta[0] * z.ctx + meta[1]
    at = place * z.shard
    chosen = where_equal((z.width, z.shard), lambda r: r, lambda c: c + at)
    for line, vector in enumerate(g_vectors):
        vector[...] = exact_dot(small[line : line + 1], chosen, 1, 0)
    at = place * z.piece
    chosen = where_equal(
        (z.width, z.piece), lambda r: jnp.bitwise_and(r, z.head - 1), lambda c: c + at
    )
    heads = g_up_bias.shape[1]
    wide = jnp.where(same_head(z, heads, z.width), small[6:7], 0.0)
    g_up_bias[...] = exact_dot(chosen, wide, 0, 1)
    for head in range(z.heads):
        wide = jnp.where(qv_lanes(z, head), small[7:8], 0.0)
        g_qv[head] = exact_dot(wide, chosen, 1, 0)


def finish_second_kernel(z, *refs):
    blocks, (g_up, g_down_t) = refs[: z.ctx], refs[z.ctx :]
    up, down = blocks[0][0].astype(F32), blocks[0][1].astype(F32)
    for block in blocks[1:]:
        up = up + block[0].astype(F32)
        down = down + block[1].astype(F32)
    g_up[...] = up
    g_down_t[...] = down


def share_kernel(z, order, *refs):
    meta, kept, got = refs[:3]
    own, sends, work = refs[3], refs[4:-1], refs[-1]
    work[...] = (kept[...].astype(F32) + got[...].astype(F32)).astype(BF)
    for step, out in zip([0] + order, (own,) + tuple(sends)):
        start = lax.rem(meta[1] + step, z.ctx) * z.shard
        out[: z.shard, :] = work[aligned(start, z.shard), :]
        out[z.shard :, :] = work[z.ctx * z.shard :, :]


def gather_blocks(order, shard):
    found = []
    for step in [0] + order:
        block = ring(shard, "ctx", step) if step else shard
        found += [block, ring(block, "fsdp", 1)]
    return found


def sum_rows(z, kept, sent):
    total = kept + flip(sent, "tp", 1).astype(F32)
    bit = 2
    while bit < z.tp:
        mine = total.astype(BF)
        total = mine.astype(F32) + flip(mine, "tp", bit).astype(F32)
        bit *= 2
    total = total.astype(BF)
    return total, flip(total, "tp", 1)


def reduce_shared(z, order, meta, kept, sent):
    got = ring(sent, "fsdp", 1)
    shape = kept.shape[:-2] + (kept.shape[-2] - (z.ctx - 1) * z.shard, kept.shape[-1])
    pieces = call(
        functools.partial(share_kernel, z, order),
        [(shape, BF)] * z.ctx,
        (kept, got),
        smem=(meta,),
        scratch=[pltpu.VMEM(kept.shape, BF)],
    )
    return send_pieces(order, pieces)


def send_pieces(order, pieces):
    got = [ring(piece, "ctx", step) for step, piece in zip(order, pieces[1:])]
    return [pieces[0]] + got


def body(
    tokens,
    lengths,
    qkv_weight,
    qv_bias,
    out_weight,
    out_bias,
    norm1_gain,
    norm1_bias,
    up_weight,
    up_bias,
    down_weight,
    down_bias,
    norm2_gain,
    norm2_bias,
    cotangent,
):
    z = Sizes(tokens, qv_bias, up_weight)
    rows = tokens.reshape(-1, z.width)
    row, col, lane = (lax.axis_index(a).astype(jnp.int32) for a in ("fsdp", "ctx", "tp"))
    meta = jnp.stack([row, col, lane])
    place = row * z.ctx + col
    order = near_first(z.ctx)
    full = (z.rows, z.width)
    half = (z.half, z.width)
    square = (z.width, z.width)

    vectors = (out_bias, norm1_gain, norm1_bias, down_bias, norm2_gain, norm2_bias)
    if z.direct:
        first_pack, token_share = call(
            functools.partial(pack_kernel, z),
            [((z.shard + TAIL, z.width), BF), ((z.rows // z.tp, z.width), BF)],
            (
                qkv_weight,
                out_weight,
                up_bias.T,
                qv_bias.transpose(1, 0, 2),
                rows,
                *(vector.reshape(1, z.shard) for vector in vectors),
            ),
            smem=(meta,),
            spare=58 << 20,
        )
    else:
        mixed_shard, tail = pack_plain(
            z, place, qkv_weight, out_weight, jnp.stack(vectors), up_bias, qv_bias
        )
        share = z.rows // z.tp
        token_share = lax.dynamic_slice_in_dim(rows, lane * share, share, 0)
    got = jnp.stack([ring(token_share, "ctx", step) for step in order])
    pieces, masks = [got], [0]
    bit = z.tp // 2
    while bit:
        pieces = pieces + [flip(piece, "tp", bit) for piece in pieces]
        masks = masks + [mask ^ bit for mask in masks]
        bit //= 2
    second_pack = jnp.concatenate([up_weight, down_weight.T], axis=0)
    if z.direct:
        first_blocks = gather_blocks(order, first_pack)
        second_blocks = gather_blocks(order, second_pack)
    else:
        split = ("fsdp", "ctx")
        mixed_all = lax.all_gather(mixed_shard, split, axis=0, tiled=True)
        tail_all = jnp.sum(lax.all_gather(tail, split, axis=0).astype(F32), axis=0).astype(BF)
        first_blocks = [jnp.concatenate([mixed_all, tail_all], axis=0)]
        second_all = lax.all_gather(second_pack, split, axis=0)
        second_all = second_all.reshape(z.blocks, 2, z.shard, z.hidden).transpose(1, 0, 2, 3)
        second_blocks = [second_all.reshape(2 * z.width, z.hidden)]

    mixed, small, every, keys, query, probs, att, kept, sent = call(
        functools.partial(attention_kernel, z, order, masks),
        [
            (square, BF),
            ((TAIL, z.width), F32),
            ((z.ctx,) + full, BF),
            ((z.seqs, z.total, z.pair), BF),
            ((z.rows, z.pair), BF),
            ((z.seqs * z.heads, z.local, z.total), BF),
            ((z.rows, z.pair), BF),
            (half, F32),
            (half, BF),
        ],
        (*first_blocks, rows, *pieces),
        smem=(meta, lengths),
        scratch=[pltpu.VMEM(full, F32)],
        flops=4 * z.rows * z.ctx * z.width * z.pair,
    )
    own, other = sum_rows(z, kept, sent)
    shown = ((z.rows, z.width // 2 + z.hidden), BF)
    up, down, normed_one, inverse_one, middle_b, slope, active, kept, sent, acts = call(
        functools.partial(forward_kernel, z, order),
        [
            (square, BF),
            (square, BF),
            (full, F32),
            ((z.rows, 1), F32),
            (full, BF),
            (full, F32),
            (full, BF),
            (half, F32),
            (half, BF),
            shown,
        ],
        (own, other, rows, small, *second_blocks),
        smem=(meta,),
        scratch=[pltpu.VMEM(full, F32)],
        flops=4 * z.rows * z.width * z.hidden,
    )
    own, other = sum_rows(z, kept, sent)
    output, d_two, d_two_b, d_pre_b, kept, sent, sums, grads = call(
        functools.partial(middle_kernel, z),
        [
            (full, BF),
            (full, F32),
            (full, BF),
            (full, BF),
            (half, F32),
            (half, BF),
            ((TAIL, z.width), F32),
            shown,
        ],
        (own, other, normed_one, small, cotangent.reshape(full), up, down, slope),
        smem=(meta,),
        scratch=[pltpu.VMEM(full, F32)],
        flops=4 * z.rows * z.width * z.hidden,
    )
    grad_args = (middle_b, d_pre_b, d_two_b, active)
    grad_flops = 4 * z.rows * z.width * z.hidden
    if z.direct:
        acts = ring(acts, "fsdp", 1)
        grads = ring(grads, "fsdp", 1)
        second = call(
            functools.partial(second_grad_kernel, z, order),
            [((2, z.shard, z.hidden), BF)] * z.ctx,
            (*grad_args, acts, grads),
            smem=(meta,),
            scratch=[pltpu.VMEM((2, z.width // 2, z.hidden), BF)],
            flops=grad_flops,
        )
        second = send_pieces(order, second)
    else:
        (second_grads,) = call(
            second_grad_whole_kernel,
            [((2,) + square, BF)],
            grad_args,
            smem=(meta,),
            flops=grad_flops,
        )
    own, other = sum_rows(z, kept, sent)
    terms_of = (z.ctx, z.half, z.width)
    d_one, d_one_b, d_query, d_keys, sums, kept, sent = call(
        functools.partial(backward_kernel, z),
        [
            (full, F32),
            (full, BF),
            ((z.rows, z.pair), BF),
            ((z.ctx, z.rows, z.pair), BF),
            ((TAIL, z.width), F32),
            (terms_of, F32),
            (terms_of, BF),
        ],
        (own, other, d_two, normed_one, inverse_one, small, mixed, att, query, keys, probs, sums),
        smem=(meta,),
        scratch=[
            pltpu.VMEM(full, F32),
            pltpu.VMEM((z.total, z.pair), F32),
            pltpu.VMEM((z.ctx,) + full, F32),
        ],
        flops=10 * z.rows * z.heads * z.total * z.pair,
    )
    terms_of = (z.ctx, z.half // 2, z.width)
    near, far = call(
        functools.partial(cut_kernel, z),
        [(terms_of, F32), (terms_of, BF)],
        (kept, flip(sent, "tp", 1)),
        smem=(meta,),
    )
    quarter = terms_of[1:]
    total, *sends = call(
        functools.partial(spread_kernel, z, order),
        [(quarter, F32)] + [(quarter, BF)] * (z.ctx - 1),
        (near, flip(far, "tp", 2)),
        smem=(meta,),
    )
    for step, piece in zip(order, sends):
        total = total + ring(piece, "ctx", step).astype(F32)
    total = total.astype(BF)
    backs = [total, flip(total, "tp", 2)]
    backs += [flip(piece, "tp", 1) for piece in backs]
    if z.direct:
        part = (z.width // 2 + TAIL, z.width)
        grad_outs = [(part, BF), (part, BF)]
    else:
        grad_outs = [(square, BF)]
    first_parts = call(
        functools.partial(first_grad_kernel, z),
        grad_outs,
        (rows, every, d_query, d_keys, d_one_b, att, sums),
        smem=(meta,),
        scratch=[pltpu.VMEM(square, BF)],
        flops=2 * z.rows * (z.ctx + 2) * z.width * z.pair,
    )
    (token_grad,) = call(
        functools.partial(token_kernel, z, [0, 2, 1, 3]),
        [(full, BF)],
        (*backs, d_one),
        smem=(meta,),
    )

    if z.direct:
        first = reduce_shared(z, order, meta, *first_parts)
        g_up, g_down_t = call(
            functools.partial(finish_second_kernel, z),
            [(up_weight.shape, F32), (up_weight.shape, F32)],
            second,
        )
        g_down = g_down_t.T
        g_qkv, g_out, g_up_bias, g_qv, *g_vectors = call(
            functools.partial(finish_first_kernel, z),
            [
                (qkv_weight.shape, F32),
                (out_weight.shape, F32),
                (up_bias.shape[::-1], F32),
                ((z.heads, 2, z.piece), F32),
            ]
            + [((1, z.shard), F32)] * 6,
            first,
            smem=(meta,),
        )
        g_up_bias = g_up_bias.T
        g_qv = g_qv.transpose(1, 0, 2)
        g_vectors = [vector.reshape(z.shard) for vector in g_vectors]
    else:
        split = ("fsdp", "ctx")
        second = lax.psum_scatter(
            second_grads.astype(F32), split, scatter_dimension=1, tiled=True
        )
        g_up, g_down = second[0], second[1].T
        g_mixed = lax.psum_scatter(
            first_parts[0].astype(F32), split, scatter_dimension=0, tiled=True
        )
        g_small = lax.psum(sums, split)
        inner = z.inner
        starts = (0, 2 * inner, 3 * inner)
        g_qkv = jnp.stack([g_mixed[:, start : start + inner] for start in starts])
        g_out = g_mixed[:, inner : 2 * inner].T
        g_vectors = lax.dynamic_slice(g_small, (0, place * z.shard), (6, z.shard))
        g_up_bias = lax.dynamic_slice(
            g_small[6].reshape(up_bias.shape[0], z.head), (0, place * z.piece), up_bias.shape
        )
        g_qv = lax.dynamic_slice(
            g_small[7, : z.pair].reshape(2, z.heads, z.head),
            (0, 0, place * z.piece),
            qv_bias.shape,
        )
    return (
        output.reshape(tokens.shape),
        token_grad.reshape(tokens.shape),
        g_qkv,
        g_qv,
        g_out,
        g_vectors[0],
        g_vectors[1],
        g_vectors[2],
        g_up,
        g_up_bias,
        g_down,
        g_vectors[3],
        g_vectors[4],
        g_vectors[5],
    )


def solution(mesh):
    split = ("fsdp", "ctx")
    vector = P(split)
    rows = P("fsdp", "ctx", None)
    weights = (
        P(None, split, "tp"),
        P(None, "tp", split),
        P("tp", split),
        vector,
        vector,
        vector,
        P(split, "tp"),
        P("tp", split),
        P("tp", split),
        vector,
        vector,
        vector,
    )

    return jax.shard_map(
        body,
        mesh=mesh,
        in_specs=(rows, P("fsdp", None)) + weights + (rows,),
        out_specs=(rows, rows) + weights,
        check_vma=False,
    )
```

```python
import functools
import math

import jax
import jax.numpy as jnp
from jax import lax
from jax.experimental import pallas as pl
from jax.experimental.pallas import tpu as pltpu
from jax.sharding import PartitionSpec as P


EPSILON = 1e-12
BF = jnp.bfloat16
F32 = jnp.float32
TAIL = 8
SPARE = 8 << 20


def norm_rows(hidden):
    center = hidden - jnp.mean(hidden, axis=-1, keepdims=True)
    inverse = lax.rsqrt(jnp.mean(center * center, axis=-1, keepdims=True) + EPSILON)
    return (center * inverse, inverse)


def norm_back(grad_norm, normed, inverse):
    first_mean = jnp.mean(grad_norm, axis=-1, keepdims=True)
    second_mean = jnp.mean(grad_norm * normed, axis=-1, keepdims=True)
    return inverse * (grad_norm - first_mean - normed * second_mean)


def gelu_parts(pre_act):
    cdf_part = 0.5 * (1.0 + lax.erf(pre_act * (1.0 / math.sqrt(2.0))))
    density = jnp.exp(-0.5 * pre_act * pre_act) * (1.0 / math.sqrt(2.0 * math.pi))
    return (pre_act * cdf_part, cdf_part + pre_act * density)


def dot(left, right, over_left, over_right):
    return lax.dot_general(
        left, right, (((over_left,), (over_right,)), ((), ())), preferred_element_type=F32
    )


def ring(value, axis, step):
    size = lax.axis_size(axis)
    return lax.ppermute(value, axis, [(i, (i + step) % size) for i in range(size)])


def flip(value, axis, bit):
    size = lax.axis_size(axis)
    return lax.ppermute(value, axis, [(i, i ^ bit) for i in range(size)])


def near_first(size):
    return sorted(range(1, size), key=lambda k: min(k, size - k))


def call(kernel, outs, args, smem=(), scratch=(), flops=0, spare=SPARE):
    size = sum(math.prod(s) * jnp.dtype(t).itemsize for s, t in outs)
    size += sum(a.size * a.dtype.itemsize for a in args)
    vmem = pl.BlockSpec(memory_space=pltpu.VMEM)
    table = pl.BlockSpec(memory_space=pltpu.SMEM)
    return pallas(kernel, outs, args, smem, scratch, flops, size, vmem, table, spare)


def pallas(kernel, outs, args, smem, scratch, flops, size, vmem, table, spare):
    held = sum(math.prod(s.shape) * jnp.dtype(s.dtype).itemsize for s in scratch)
    room = size + held + spare
    return pl.pallas_call(
        kernel,
        out_shape=tuple(jax.ShapeDtypeStruct(s, t) for s, t in outs),
        in_specs=[table] * len(smem) + [vmem] * len(args),
        out_specs=tuple(vmem for _ in outs),
        scratch_shapes=list(scratch),
        compiler_params=pltpu.CompilerParams(vmem_limit_bytes=room),
        cost_estimate=pl.CostEstimate(flops=flops, bytes_accessed=size, transcendentals=0),
    )(*smem, *args)


def lanes(low, high, width):
    at = lax.broadcasted_iota(jnp.int32, (1, width), 1)
    return (at >= low) & (at < high)


def aligned(start, size):
    return pl.ds(pl.multiple_of(start, size), size)


class Sizes:
    def __init__(self, tokens, qv_bias, up_weight):
        self.seqs, self.local, self.width = tokens.shape
        self.rows = self.seqs * self.local
        self.fsdp, self.ctx, self.tp = (lax.axis_size(a) for a in ("fsdp", "ctx", "tp"))
        self.blocks = self.fsdp * self.ctx
        self.shard = self.width // self.blocks
        self.heads, self.piece = qv_bias.shape[1:]
        self.head = self.piece * self.blocks
        self.inner = self.heads * self.head
        self.pair = 2 * self.inner
        self.hidden = up_weight.shape[1]
        self.total = self.local * self.ctx
        self.half = self.rows // 2
        self.scale = 1.0 / math.sqrt(self.head)
        self.folded = self.ctx == 4
        self.direct = self.fsdp == 2 and self.shard % 16 == 0


def attention_kernel(z, order, masks, *refs):
    (meta, lengths), refs = refs[:2], refs[2:]
    count = z.blocks if z.direct else 1
    blocks, refs = refs[:count], refs[count:]
    own, refs = refs[0], refs[1:]
    pieces, refs = refs[: len(masks)], refs[len(masks) :]
    mixed, small, every, keys, query, probs, att, kept, sent = refs[:9]
    part = refs[9]
    row, col, lane = meta[0], meta[1], meta[2]
    if z.direct:
        places = block_places(z, order, row, col)
        total = jnp.zeros((TAIL, z.width), F32)
        for block, place in zip(blocks, places):
            mixed[aligned(place * z.shard, z.shard), :] = block[: z.shard, :]
            total = total + block[z.shard :, :].astype(F32)
        small[...] = total
    else:
        mixed[...] = blocks[0][: z.width, :]
        small[...] = blocks[0][z.width :, :].astype(F32)
    every[col] = own[...]
    share = z.rows // z.tp
    for at, step in enumerate(order):
        source = lax.rem(col - step + z.ctx, z.ctx)
        for which, mask in enumerate(masks):
            spot = jnp.bitwise_xor(lane, mask) * share
            every[source, aligned(spot, share), :] = pieces[which][at]
    b_q = jnp.where(lanes(0, z.inner, z.pair), small[7:8, : z.pair], 0.0)
    b_kv = jnp.where(lanes(z.inner, z.pair, z.pair), small[7:8, : z.pair], 0.0)

    @pl.loop(0, z.ctx)
    def _(at):
        both = dot(every[at], mixed[:, z.pair :], 1, 0) + b_kv
        both = both.astype(BF)
        for seq in range(z.seqs):
            piece = both[seq * z.local : (seq + 1) * z.local]
            keys[seq, aligned(at * z.local, z.local), :] = piece

    flat = dot(own[...], mixed[:, : z.pair], 1, 0) + b_q
    query[...] = jnp.where(lanes(0, z.inner, z.pair), flat, 0.0).astype(BF)
    docs = lengths.shape[1]
    key_at = lax.broadcasted_iota(jnp.int32, (1, z.total), 1)
    query_at = lax.broadcasted_iota(jnp.int32, (z.local, 1), 0) + col * z.local
    for seq in range(z.seqs):
        key_label = jnp.zeros((1, z.total), jnp.int32)
        query_label = jnp.zeros((z.local, 1), jnp.int32)
        end = 0
        for doc in range(docs):
            end = end + lengths[seq, doc]
            key_label = key_label + jnp.where(key_at >= end, 1, 0)
            query_label = query_label + jnp.where(query_at >= end, 1, 0)
        same = query_label == key_label
        flat = query[seq * z.local : (seq + 1) * z.local, :]
        result = jnp.zeros((z.local, z.pair), F32)
        for head in range(z.heads):
            low = head * z.head
            chosen = jnp.where(lanes(low, low + z.head, z.pair), flat, jnp.zeros_like(flat))
            scores = dot(chosen, keys[seq], 1, 1) * z.scale
            scores = jnp.where(same, scores, -1e30)
            weights = jnp.exp(scores - jnp.max(scores, axis=1, keepdims=True))
            chance = weights * (1.0 / jnp.sum(weights, axis=1, keepdims=True))
            chance = chance.astype(BF)
            probs[seq * z.heads + head] = chance
            low = low + z.inner
            found = dot(chance, keys[seq], 1, 0)
            result = jnp.where(lanes(low, low + z.head, z.pair), found, result)
        att[seq * z.local : (seq + 1) * z.local, :] = result.astype(BF)
    part[...] = dot(att[...], mixed[:, : z.pair], 1, 1)
    split_halves(z, lane, part, kept, sent)


def block_places(z, order, row, col):
    places = []
    for step in [0] + order:
        source = lax.rem(col - step + z.ctx, z.ctx)
        places.append(row * z.ctx + source)
        places.append((1 - row) * z.ctx + source)
    return places


def split_halves(z, lane, part, kept, sent):
    parity = jnp.bitwise_and(lane, 1)
    kept[...] = part[aligned(parity * z.half, z.half), :]
    sent[...] = part[aligned((1 - parity) * z.half, z.half), :].astype(sent.dtype)


def place_halves(z, lane, own, other, whole):
    parity = jnp.bitwise_and(lane, 1)
    whole[aligned(parity * z.half, z.half), :] = own[...].astype(F32)
    whole[aligned((1 - parity) * z.half, z.half), :] = other[...].astype(F32)


def forward_kernel(z, order, *refs):
    meta, own, other, rows, small = refs[:5]
    count = z.blocks if z.direct else 1
    blocks, refs = refs[5 : 5 + count], refs[5 + count :]
    up, down, normed_one, inverse_one, middle_b, slope, active, kept, sent, shown = refs[:10]
    work = refs[10]
    row, col, lane = meta[0], meta[1], meta[2]
    if z.direct:
        for block, place in zip(blocks, block_places(z, order, row, col)):
            up[aligned(place * z.shard, z.shard), :] = block[: z.shard, :]
            down[aligned(place * z.shard, z.shard), :] = block[z.shard :, :]
    else:
        up[...] = blocks[0][: z.width, :]
        down[...] = blocks[0][z.width :, :]
    place_halves(z, lane, own, other, work)
    hidden = rows[...].astype(F32) + work[...] + small[0:1, :]
    normed, inverse = norm_rows(hidden)
    normed_one[...] = normed
    inverse_one[...] = inverse
    middle_b[...] = (normed * small[1:2, :] + small[2:3, :]).astype(BF)
    pre = dot(middle_b[...], up[...], 1, 0) + small[6:7, :]
    activated, gradient = gelu_parts(pre)
    slope[...] = gradient
    active[...] = activated.astype(BF)
    show(z, row, middle_b, active, shown)
    work[...] = dot(active[...], down[...], 1, 1)
    split_halves(z, lane, work, kept, sent)


def show(z, row, columns, whole, shown):
    part = z.width // 2
    shown[:, :part] = half_columns(z, 1 - row, columns)
    shown[:, part:] = whole[...]


def half_columns(z, which, columns):
    part = z.width // 2
    return jnp.where(which == 0, columns[:, :part], columns[:, part:])


def middle_kernel(z, *refs):
    meta, own, other, normed_one, small, cotangent, up, down, slope = refs[:9]
    output, d_two, d_two_b, d_pre_b, kept, sent, sums, shown, work = refs[9:]
    lane = meta[2]
    place_halves(z, lane, own, other, work)
    middle = normed_one[...] * small[1:2, :] + small[2:3, :]
    normed, inverse = norm_rows(middle + work[...] + small[3:4, :])
    output[...] = (normed * small[4:5, :] + small[5:6, :]).astype(BF)
    grad_in = cotangent[...].astype(F32)
    sums[...] = jnp.zeros_like(sums)
    sums[4:5, :] = jnp.sum(grad_in * normed, axis=0, keepdims=True)
    sums[5:6, :] = jnp.sum(grad_in, axis=0, keepdims=True)
    d_res = norm_back(grad_in * small[4:5, :], normed, inverse)
    sums[3:4, :] = jnp.sum(d_res, axis=0, keepdims=True)
    d_two[...] = d_res
    d_two_b[...] = d_res.astype(BF)
    d_pre = dot(d_two_b[...], down[...], 1, 0) * slope[...]
    sums[6:7, :] = jnp.sum(d_pre, axis=0, keepdims=True)
    d_pre_b[...] = d_pre.astype(BF)
    show(z, meta[0], d_two_b, d_pre_b, shown)
    work[...] = dot(d_pre_b[...], up[...], 1, 1)
    split_halves(z, lane, work, kept, sent)


def second_grad_kernel(z, order, *refs):
    meta, middle_b, d_pre_b, d_two_b, active, acts, grads = refs[:7]
    outs, work = refs[7:-1], refs[-1]
    part = z.width // 2
    total = dot(half_columns(z, meta[0], middle_b), d_pre_b[...], 0, 0)
    total = total + dot(acts[:, :part], grads[:, part:], 0, 0)
    work[0] = total.astype(BF)
    total = dot(half_columns(z, meta[0], d_two_b), active[...], 0, 0)
    total = total + dot(grads[:, :part], acts[:, part:], 0, 0)
    work[1] = total.astype(BF)
    for start, out in zip(block_starts(z, order, meta[1]), outs):
        for at in range(2):
            out[at] = work[at, aligned(start, z.shard), :]


def second_grad_whole_kernel(*refs):
    _, middle_b, d_pre_b, d_two_b, active, out = refs
    out[0] = dot(middle_b[...], d_pre_b[...], 0, 0).astype(BF)
    out[1] = dot(d_two_b[...], active[...], 0, 0).astype(BF)


def backward_kernel(z, *refs):
    (meta, own, other, d_two, normed_one, inverse_one, small, mixed, att, query, keys), refs = (
        refs[:11],
        refs[11:],
    )
    (probs, sums_in), refs = refs[:2], refs[2:]
    d_one, d_one_b, d_query, d_keys, sums, kept, sent = refs[:7]
    work, grads, back = refs[7:]
    col, lane = meta[1], meta[2]
    place_halves(z, lane, own, other, work)
    d_middle = d_two[...] + work[...]
    normed = normed_one[...]
    sums[...] = sums_in[...]
    sums[1:2, :] = jnp.sum(d_middle * normed, axis=0, keepdims=True)
    sums[2:3, :] = jnp.sum(d_middle, axis=0, keepdims=True)
    d_res = norm_back(d_middle * small[1:2, :], normed, inverse_one[...])
    sums[0:1, :] = jnp.sum(d_res, axis=0, keepdims=True)
    d_one[...] = d_res
    d_one_b[...] = d_res.astype(BF)
    upper = lanes(z.inner, z.pair, z.pair)
    d_att = jnp.where(upper, dot(d_one_b[...], mixed[:, : z.pair], 1, 0), 0.0).astype(BF)
    qv_sum = jnp.zeros((1, z.pair), F32)
    for seq in range(z.seqs):
        span = slice(seq * z.local, (seq + 1) * z.local)
        d_here, a_here, q_here = d_att[span], att[span, :], query[span, :]
        product = d_here.astype(F32) * a_here.astype(F32)
        d_q = jnp.zeros((z.local, z.pair), F32)
        for head in range(z.heads):
            low = head * z.head
            near = lanes(low, low + z.head, z.pair)
            far = lanes(low + z.inner, low + z.inner + z.head, z.pair)
            q_head = jnp.where(near, q_here, jnp.zeros_like(q_here))
            d_head = jnp.where(far, d_here, jnp.zeros_like(d_here))
            delta = jnp.sum(jnp.where(far, product, 0.0), axis=1, keepdims=True)
            chance = probs[seq * z.heads + head]
            d_chance = dot(d_head, keys[seq], 1, 1)
            d_scores = (chance.astype(F32) * (d_chance - delta)).astype(BF)
            d_q = jnp.where(near, dot(d_scores, keys[seq], 1, 0), d_q)
            d_kv = dot(d_scores, q_head, 0, 0) * z.scale + dot(chance, d_head, 0, 0)
            if head == 0:
                grads[...] = d_kv
            else:
                grads[...] += d_kv
        d_q = d_q * z.scale
        qv_sum = qv_sum + jnp.sum(d_q, axis=0, keepdims=True)
        qv_sum = qv_sum + jnp.where(upper, jnp.sum(grads[...], axis=0, keepdims=True), 0.0)
        d_query[span, :] = d_q.astype(BF)
        for at in range(z.ctx):
            d_keys[at, span, :] = grads[at * z.local : (at + 1) * z.local, :].astype(BF)
    sums[7:8, : z.pair] = qv_sum
    for at in range(z.ctx):
        back[at] = dot(d_keys[at], mixed[:, z.pair :], 1, 1)
    back[col] += dot(d_query[...], mixed[:, : z.pair], 1, 1)
    parity = jnp.bitwise_and(lane, 1)
    kept[...] = back[:, aligned(parity * z.half, z.half), :]
    sent[...] = back[:, aligned((1 - parity) * z.half, z.half), :].astype(BF)


def first_grad_kernel(z, *refs):
    meta, rows, every, d_query, d_keys, d_one_b, att, sums = refs[:8]
    outs, work = refs[8:-1], refs[-1]
    near = dot(rows[...], d_query[...], 0, 0) + dot(d_one_b[...], att[...], 0, 0)
    work[:, : z.pair] = near.astype(BF)
    far = dot(every[0], d_keys[0], 0, 0)
    for at in range(1, z.ctx):
        far = far + dot(every[at], d_keys[at], 0, 0)
    work[:, z.pair :] = far.astype(BF)
    if len(outs) == 1:
        outs[0][...] = work[...]
        return
    part = z.width // 2
    for out, start in zip(outs, (meta[0] * part, (1 - meta[0]) * part)):
        out[:part, :] = work[aligned(start, part), :]
        out[part:, :] = sums[...].astype(BF)


def cut_kernel(z, meta, kept, got, near, far):
    chip = lax.shift_right_logical(meta[2], 1)
    size = z.half // 2
    for out, which in ((near, chip), (far, 1 - chip)):
        span = aligned(which * size, size)
        out[...] = (kept[:, span, :] + got[:, span, :].astype(F32)).astype(out.dtype)


def spread_kernel(z, order, meta, kept, got, own, *sends):
    for step, out in zip([0] + order, (own,) + sends):
        at = lax.rem(meta[1] + step, z.ctx)
        out[...] = (kept[at] + got[at].astype(F32)).astype(out.dtype)


def token_kernel(z, masks, meta, *refs):
    pieces, (d_one, out) = refs[:-2], refs[-2:]
    size = z.rows // z.tp
    for mask, piece in zip(masks, pieces):
        lane = jnp.bitwise_xor(meta[2], mask)
        start = jnp.bitwise_and(lane, 1) * z.half + lax.shift_right_logical(lane, 1) * size
        span = aligned(start, size)
        out[span, :] = (d_one[span, :] + piece[...].astype(F32)).astype(BF)


def where_equal(shape, left, right):
    rows = lax.broadcasted_iota(jnp.int32, shape, 0)
    cols = lax.broadcasted_iota(jnp.int32, shape, 1)
    return jnp.where(left(rows) == right(cols), 1.0, 0.0).astype(BF)


def same_head(z, heads, width):
    rows = lax.broadcasted_iota(jnp.int32, (heads, width), 0)
    cols = lax.broadcasted_iota(jnp.int32, (heads, width), 1)
    return (cols >= rows * z.head) & (cols < (rows + 1) * z.head)


def qv_lanes(z, head):
    start = lax.broadcasted_iota(jnp.int32, (2, z.width), 0) * z.inner + head * z.head
    cols = lax.broadcasted_iota(jnp.int32, (2, z.width), 1)
    return (cols >= start) & (cols < start + z.head)


def pack_kernel(z, *refs):
    meta, qkv, out, up_bias, qv_bias, rows = refs[:6]
    vectors, (pack, share) = refs[6:-2], refs[-2:]
    place = meta[0] * z.ctx + meta[1]
    inner = z.inner

    def spread(at):
        return where_equal((inner, z.width), lambda r: r + at * inner, lambda c: c)

    total = dot(qkv[0], spread(0), 1, 0) + dot(out[...], spread(1), 0, 0)
    total = total + dot(qkv[1], spread(2), 1, 0) + dot(qkv[2], spread(3), 1, 0)
    pack[: z.shard, :] = total.astype(BF)
    at = place * z.shard
    chosen = where_equal((z.shard, z.width), lambda r: r + at, lambda c: c)
    lines = [dot(vector[...], chosen, 1, 0) for vector in vectors]
    at = place * z.piece
    chosen = where_equal(
        (z.piece, z.width), lambda r: r + at, lambda c: jnp.bitwise_and(c, z.head - 1)
    )
    heads = up_bias.shape[1]
    wide = jnp.where(same_head(z, heads, z.width), dot(up_bias[...], chosen, 0, 0), 0.0)
    lines.append(jnp.sum(wide, axis=0, keepdims=True))
    line = jnp.zeros((1, z.width), F32)
    for head in range(z.heads):
        wide = jnp.where(qv_lanes(z, head), dot(qv_bias[head], chosen, 1, 0), 0.0)
        line = line + jnp.sum(wide, axis=0, keepdims=True)
    lines.append(line)
    pack[z.shard :, :] = jnp.concatenate(lines, axis=0).astype(BF)
    size = z.rows // z.tp
    share[...] = rows[aligned(meta[2] * size, size), :]


def pack_plain(z, place, qkv_weight, out_weight, vectors, up_bias, qv_bias):
    vectors = lax.dynamic_update_slice(jnp.zeros((6, z.width), BF), vectors, (0, place * z.shard))
    up_row = lax.dynamic_update_slice(
        jnp.zeros((up_bias.shape[0], z.head), BF), up_bias, (0, place * z.piece)
    ).reshape(1, z.hidden)
    qv_row = lax.dynamic_update_slice(
        jnp.zeros((2, z.heads, z.head), BF), qv_bias, (0, 0, place * z.piece)
    ).reshape(1, z.pair)
    qv_row = jnp.pad(qv_row, ((0, 0), (0, z.width - z.pair)))
    tail = jnp.concatenate([vectors, up_row, qv_row], axis=0)
    mixed = jnp.concatenate([qkv_weight[0], out_weight.T, qkv_weight[1], qkv_weight[2]], axis=1)
    return mixed, tail


def terms(value):
    high = value.astype(BF)
    rest = value - high.astype(F32)
    middle = rest.astype(BF)
    return high, middle, (rest - middle.astype(F32)).astype(BF)


def exact_dot(left, right, over_left, over_right):
    if left.dtype == F32:
        return sum(dot(term, right, over_left, over_right) for term in terms(left))
    return sum(dot(left, term, over_left, over_right) for term in terms(right))


def finish_first_kernel(z, meta, *refs):
    blocks, refs = refs[: z.ctx], refs[z.ctx :]
    (g_qkv, g_out, g_up_bias, g_qv), g_vectors = refs[:4], refs[4:]
    total = blocks[0][...].astype(F32)
    for block in blocks[1:]:
        total = total + block[...].astype(F32)
    inner = z.inner
    for at, start in enumerate((0, 2 * inner, 3 * inner)):
        g_qkv[at] = total[: z.shard, start : start + inner]
    eye = where_equal((z.shard, z.shard), lambda r: r, lambda c: c)
    g_out[...] = exact_dot(total[: z.shard, inner : 2 * inner], eye, 0, 0)
    small = total[z.shard :]
    place = meta[0] * z.ctx + meta[1]
    at = place * z.shard
    chosen = where_equal((z.width, z.shard), lambda r: r, lambda c: c + at)
    found = exact_dot(small, chosen, 1, 0)
    for line, vector in enumerate(g_vectors):
        vector[...] = found[line : line + 1]
    at = place * z.piece
    chosen = where_equal(
        (z.width, z.piece), lambda r: jnp.bitwise_and(r, z.head - 1), lambda c: c + at
    )
    heads = g_up_bias.shape[1]
    wide = jnp.where(same_head(z, heads, z.width), small[6:7], 0.0)
    g_up_bias[...] = exact_dot(chosen, wide, 0, 1)
    wide = [jnp.where(qv_lanes(z, head), small[7:8], 0.0) for head in range(z.heads)]
    found = exact_dot(jnp.concatenate(wide, axis=0), chosen, 1, 0)
    for head in range(z.heads):
        g_qv[head] = found[2 * head : 2 * head + 2]


def finish_second_kernel(z, *refs):
    blocks, (g_up, g_down_t) = refs[: z.ctx], refs[z.ctx :]
    up, down = blocks[0][0].astype(F32), blocks[0][1].astype(F32)
    for block in blocks[1:]:
        up = up + block[0].astype(F32)
        down = down + block[1].astype(F32)
    g_up[...] = up
    g_down_t[...] = down


def share_kernel(z, order, *refs):
    meta, kept, got = refs[:3]
    outs, work = refs[3:-1], refs[-1]
    work[...] = (kept[...].astype(F32) + got[...].astype(F32)).astype(BF)
    for start, out in zip(block_starts(z, order, meta[1]), outs):
        out[: z.shard, :] = work[aligned(start, z.shard), :]
        out[z.shard :, :] = work[z.ctx * z.shard :, :]


def gather_blocks(order, shard):
    found = []
    for step in [0] + order:
        block = ring(shard, "ctx", step) if step else shard
        found += [block, ring(block, "fsdp", 1)]
    return found


def sum_rows(z, kept, sent):
    total = kept + flip(sent, "tp", 1).astype(F32)
    bit = 2
    while bit < z.tp:
        mine = total.astype(BF)
        total = mine.astype(F32) + flip(mine, "tp", bit).astype(F32)
        bit *= 2
    total = total.astype(BF)
    return total, flip(total, "tp", 1)


def reduce_shared(z, order, meta, kept, sent):
    got = ring(sent, "fsdp", 1)
    shape = kept.shape[:-2] + (kept.shape[-2] - (z.ctx - 1) * z.shard, kept.shape[-1])
    pieces = call(
        functools.partial(share_kernel, z, order),
        [(shape, BF)] * (z.ctx + z.folded),
        (kept, got),
        smem=(meta,),
        scratch=[pltpu.VMEM(kept.shape, BF)],
    )
    return send_pieces(z, order, pieces)


def send_pieces(z, order, pieces):
    if not z.folded:
        return [pieces[0]] + [ring(piece, "ctx", step) for step, piece in zip(order, pieces[1:])]
    own, right, left, far, fold = pieces
    fold = lax.ppermute(fold, "ctx", ((0, 1), (3, 2)))
    right = lax.ppermute(right, "ctx", ((0, 1), (1, 2), (2, 3)))
    left = lax.ppermute(left, "ctx", ((1, 0), (2, 1), (3, 2)))
    far = (far.astype(F32) + fold.astype(F32)).astype(BF)
    return [own, right, left, ring(far, "ctx", 2)]


def block_starts(z, order, col):
    starts = [lax.rem(col + step, z.ctx) for step in [0] + order]
    if z.folded:
        starts.append(jnp.where(col == 0, z.ctx - 1, 0))
    return [start * z.shard for start in starts]


def body(
    tokens,
    lengths,
    qkv_weight,
    qv_bias,
    out_weight,
    out_bias,
    norm1_gain,
    norm1_bias,
    up_weight,
    up_bias,
    down_weight,
    down_bias,
    norm2_gain,
    norm2_bias,
    cotangent,
):
    z = Sizes(tokens, qv_bias, up_weight)
    rows = tokens.reshape(-1, z.width)
    row, col, lane = (lax.axis_index(a).astype(jnp.int32) for a in ("fsdp", "ctx", "tp"))
    meta = jnp.stack([row, col, lane])
    place = row * z.ctx + col
    order = near_first(z.ctx)
    full = (z.rows, z.width)
    half = (z.half, z.width)
    square = (z.width, z.width)

    vectors = (out_bias, norm1_gain, norm1_bias, down_bias, norm2_gain, norm2_bias)
    if z.direct:
        first_pack, token_share = call(
            functools.partial(pack_kernel, z),
            [((z.shard + TAIL, z.width), BF), ((z.rows // z.tp, z.width), BF)],
            (
                qkv_weight,
                out_weight,
                up_bias.T,
                qv_bias.transpose(1, 0, 2),
                rows,
                *(vector.reshape(1, z.shard) for vector in vectors),
            ),
            smem=(meta,),
            spare=58 << 20,
        )
    else:
        mixed_shard, tail = pack_plain(
            z, place, qkv_weight, out_weight, jnp.stack(vectors), up_bias, qv_bias
        )
        share = z.rows // z.tp
        token_share = lax.dynamic_slice_in_dim(rows, lane * share, share, 0)
    got = jnp.stack([ring(token_share, "ctx", step) for step in order])
    pieces, masks = [got], [0]
    bit = z.tp // 2
    while bit:
        pieces = pieces + [flip(piece, "tp", bit) for piece in pieces]
        masks = masks + [mask ^ bit for mask in masks]
        bit //= 2
    second_pack = jnp.concatenate([up_weight, down_weight.T], axis=0)
    if z.direct:
        first_blocks = gather_blocks(order, first_pack)
        second_blocks = gather_blocks(order, second_pack)
    else:
        split = ("fsdp", "ctx")
        mixed_all = lax.all_gather(mixed_shard, split, axis=0, tiled=True)
        tail_all = jnp.sum(lax.all_gather(tail, split, axis=0).astype(F32), axis=0).astype(BF)
        first_blocks = [jnp.concatenate([mixed_all, tail_all], axis=0)]
        second_all = lax.all_gather(second_pack, split, axis=0)
        second_all = second_all.reshape(z.blocks, 2, z.shard, z.hidden).transpose(1, 0, 2, 3)
        second_blocks = [second_all.reshape(2 * z.width, z.hidden)]

    mixed, small, every, keys, query, probs, att, kept, sent = call(
        functools.partial(attention_kernel, z, order, masks),
        [
            (square, BF),
            ((TAIL, z.width), F32),
            ((z.ctx,) + full, BF),
            ((z.seqs, z.total, z.pair), BF),
            ((z.rows, z.pair), BF),
            ((z.seqs * z.heads, z.local, z.total), BF),
            ((z.rows, z.pair), BF),
            (half, F32),
            (half, BF),
        ],
        (*first_blocks, rows, *pieces),
        smem=(meta, lengths),
        scratch=[pltpu.VMEM(full, F32)],
        flops=4 * z.rows * z.ctx * z.width * z.pair,
    )
    own, other = sum_rows(z, kept, sent)
    shown = ((z.rows, z.width // 2 + z.hidden), BF)
    up, down, normed_one, inverse_one, middle_b, slope, active, kept, sent, acts = call(
        functools.partial(forward_kernel, z, order),
        [
            (square, BF),
            (square, BF),
            (full, F32),
            ((z.rows, 1), F32),
            (full, BF),
            (full, F32),
            (full, BF),
            (half, F32),
            (half, BF),
            shown,
        ],
        (own, other, rows, small, *second_blocks),
        smem=(meta,),
        scratch=[pltpu.VMEM(full, F32)],
        flops=4 * z.rows * z.width * z.hidden,
    )
    own, other = sum_rows(z, kept, sent)
    output, d_two, d_two_b, d_pre_b, kept, sent, sums, grads = call(
        functools.partial(middle_kernel, z),
        [
            (full, BF),
            (full, F32),
            (full, BF),
            (full, BF),
            (half, F32),
            (half, BF),
            ((TAIL, z.width), F32),
            shown,
        ],
        (own, other, normed_one, small, cotangent.reshape(full), up, down, slope),
        smem=(meta,),
        scratch=[pltpu.VMEM(full, F32)],
        flops=4 * z.rows * z.width * z.hidden,
    )
    grad_args = (middle_b, d_pre_b, d_two_b, active)
    grad_flops = 4 * z.rows * z.width * z.hidden
    if z.direct:
        acts = ring(acts, "fsdp", 1)
        grads = ring(grads, "fsdp", 1)
        second = call(
            functools.partial(second_grad_kernel, z, order),
            [((2, z.shard, z.hidden), BF)] * (z.ctx + z.folded),
            (*grad_args, acts, grads),
            smem=(meta,),
            scratch=[pltpu.VMEM((2, z.width // 2, z.hidden), BF)],
            flops=grad_flops,
        )
        second = send_pieces(z, order, second)
    else:
        (second_grads,) = call(
            second_grad_whole_kernel,
            [((2,) + square, BF)],
            grad_args,
            smem=(meta,),
            flops=grad_flops,
        )
    own, other = sum_rows(z, kept, sent)
    terms_of = (z.ctx, z.half, z.width)
    d_one, d_one_b, d_query, d_keys, sums, kept, sent = call(
        functools.partial(backward_kernel, z),
        [
            (full, F32),
            (full, BF),
            ((z.rows, z.pair), BF),
            ((z.ctx, z.rows, z.pair), BF),
            ((TAIL, z.width), F32),
            (terms_of, F32),
            (terms_of, BF),
        ],
        (own, other, d_two, normed_one, inverse_one, small, mixed, att, query, keys, probs, sums),
        smem=(meta,),
        scratch=[
            pltpu.VMEM(full, F32),
            pltpu.VMEM((z.total, z.pair), F32),
            pltpu.VMEM((z.ctx,) + full, F32),
        ],
        flops=10 * z.rows * z.heads * z.total * z.pair,
    )
    terms_of = (z.ctx, z.half // 2, z.width)
    near, far = call(
        functools.partial(cut_kernel, z),
        [(terms_of, F32), (terms_of, BF)],
        (kept, flip(sent, "tp", 1)),
        smem=(meta,),
    )
    quarter = terms_of[1:]
    total, *sends = call(
        functools.partial(spread_kernel, z, order),
        [(quarter, F32)] + [(quarter, BF)] * (z.ctx - 1),
        (near, flip(far, "tp", 2)),
        smem=(meta,),
    )
    for step, piece in zip(order, sends):
        total = total + ring(piece, "ctx", step).astype(F32)
    total = total.astype(BF)
    backs = [total, flip(total, "tp", 2)]
    backs += [flip(piece, "tp", 1) for piece in backs]
    if z.direct:
        part = (z.width // 2 + TAIL, z.width)
        grad_outs = [(part, BF), (part, BF)]
    else:
        grad_outs = [(square, BF)]
    first_parts = call(
        functools.partial(first_grad_kernel, z),
        grad_outs,
        (rows, every, d_query, d_keys, d_one_b, att, sums),
        smem=(meta,),
        scratch=[pltpu.VMEM(square, BF)],
        flops=2 * z.rows * (z.ctx + 2) * z.width * z.pair,
    )
    (token_grad,) = call(
        functools.partial(token_kernel, z, [0, 2, 1, 3]),
        [(full, BF)],
        (*backs, d_one),
        smem=(meta,),
    )

    if z.direct:
        first = reduce_shared(z, order, meta, *first_parts)
        g_up, g_down_t = call(
            functools.partial(finish_second_kernel, z),
            [(up_weight.shape, F32), (up_weight.shape, F32)],
            second,
        )
        g_down = g_down_t.T
        g_qkv, g_out, g_up_bias, g_qv, *g_vectors = call(
            functools.partial(finish_first_kernel, z),
            [
                (qkv_weight.shape, F32),
                (out_weight.shape, F32),
                (up_bias.shape[::-1], F32),
                ((z.heads, 2, z.piece), F32),
            ]
            + [((1, z.shard), F32)] * 6,
            first,
            smem=(meta,),
        )
        g_up_bias = g_up_bias.T
        g_qv = g_qv.transpose(1, 0, 2)
        g_vectors = [vector.reshape(z.shard) for vector in g_vectors]
    else:
        split = ("fsdp", "ctx")
        second = lax.psum_scatter(
            second_grads.astype(F32), split, scatter_dimension=1, tiled=True
        )
        g_up, g_down = second[0], second[1].T
        g_mixed = lax.psum_scatter(
            first_parts[0].astype(F32), split, scatter_dimension=0, tiled=True
        )
        g_small = lax.psum(sums, split)
        inner = z.inner
        starts = (0, 2 * inner, 3 * inner)
        g_qkv = jnp.stack([g_mixed[:, start : start + inner] for start in starts])
        g_out = g_mixed[:, inner : 2 * inner].T
        g_vectors = lax.dynamic_slice(g_small, (0, place * z.shard), (6, z.shard))
        g_up_bias = lax.dynamic_slice(
            g_small[6].reshape(up_bias.shape[0], z.head), (0, place * z.piece), up_bias.shape
        )
        g_qv = lax.dynamic_slice(
            g_small[7, : z.pair].reshape(2, z.heads, z.head),
            (0, 0, place * z.piece),
            qv_bias.shape,
        )
    return (
        output.reshape(tokens.shape),
        token_grad.reshape(tokens.shape),
        g_qkv,
        g_qv,
        g_out,
        g_vectors[0],
        g_vectors[1],
        g_vectors[2],
        g_up,
        g_up_bias,
        g_down,
        g_vectors[3],
        g_vectors[4],
        g_vectors[5],
    )


def solution(mesh):
    split = ("fsdp", "ctx")
    vector = P(split)
    rows = P("fsdp", "ctx", None)
    weights = (
        P(None, split, "tp"),
        P(None, "tp", split),
        P("tp", split),
        vector,
        vector,
        vector,
        P(split, "tp"),
        P("tp", split),
        P("tp", split),
        vector,
        vector,
        vector,
    )

    return jax.shard_map(
        body,
        mesh=mesh,
        in_specs=(rows, P("fsdp", None)) + weights + (rows,),
        out_specs=(rows, rows) + weights,
        check_vma=False,
    )
```

```python
import functools
import math

import jax
import jax.numpy as jnp
from jax import lax
from jax.experimental import pallas as pl
from jax.experimental.pallas import tpu as pltpu
from jax.sharding import PartitionSpec as P


EPSILON = 1e-12
BF = jnp.bfloat16
F32 = jnp.float32
TAIL = 8
SPARE = 8 << 20


def norm_rows(hidden):
    center = hidden - jnp.mean(hidden, axis=-1, keepdims=True)
    inverse = lax.rsqrt(jnp.mean(center * center, axis=-1, keepdims=True) + EPSILON)
    return (center * inverse, inverse)


def norm_back(grad_norm, normed, inverse):
    first_mean = jnp.mean(grad_norm, axis=-1, keepdims=True)
    second_mean = jnp.mean(grad_norm * normed, axis=-1, keepdims=True)
    return inverse * (grad_norm - first_mean - normed * second_mean)


def gelu_parts(pre_act):
    cdf_part = 0.5 * (1.0 + lax.erf(pre_act * (1.0 / math.sqrt(2.0))))
    density = jnp.exp(-0.5 * pre_act * pre_act) * (1.0 / math.sqrt(2.0 * math.pi))
    return (pre_act * cdf_part, cdf_part + pre_act * density)


def dot(left, right, over_left, over_right):
    return lax.dot_general(
        left, right, (((over_left,), (over_right,)), ((), ())), preferred_element_type=F32
    )


def ring(value, axis, step):
    size = lax.axis_size(axis)
    return lax.ppermute(value, axis, [(i, (i + step) % size) for i in range(size)])


def flip(value, axis, bit):
    size = lax.axis_size(axis)
    return lax.ppermute(value, axis, [(i, i ^ bit) for i in range(size)])


def near_first(size):
    return sorted(range(1, size), key=lambda k: min(k, size - k))


def call(kernel, outs, args, smem=(), scratch=(), flops=0, spare=SPARE):
    size = sum(math.prod(s) * jnp.dtype(t).itemsize for s, t in outs)
    size += sum(a.size * a.dtype.itemsize for a in args)
    vmem = pl.BlockSpec(memory_space=pltpu.VMEM)
    table = pl.BlockSpec(memory_space=pltpu.SMEM)
    return pallas(kernel, outs, args, smem, scratch, flops, size, vmem, table, spare)


def pallas(kernel, outs, args, smem, scratch, flops, size, vmem, table, spare):
    held = sum(math.prod(s.shape) * jnp.dtype(s.dtype).itemsize for s in scratch)
    room = size + held + spare
    return pl.pallas_call(
        kernel,
        out_shape=tuple(jax.ShapeDtypeStruct(s, t) for s, t in outs),
        in_specs=[table] * len(smem) + [vmem] * len(args),
        out_specs=tuple(vmem for _ in outs),
        scratch_shapes=list(scratch),
        compiler_params=pltpu.CompilerParams(vmem_limit_bytes=room),
        cost_estimate=pl.CostEstimate(flops=flops, bytes_accessed=size, transcendentals=0),
    )(*smem, *args)


def lanes(low, high, width):
    at = lax.broadcasted_iota(jnp.int32, (1, width), 1)
    return (at >= low) & (at < high)


def aligned(start, size):
    return pl.ds(pl.multiple_of(start, size), size)


class Sizes:
    def __init__(self, tokens, qv_bias, up_weight):
        self.seqs, self.local, self.width = tokens.shape
        self.rows = self.seqs * self.local
        self.fsdp, self.ctx, self.tp = (lax.axis_size(a) for a in ("fsdp", "ctx", "tp"))
        self.blocks = self.fsdp * self.ctx
        self.shard = self.width // self.blocks
        self.heads, self.piece = qv_bias.shape[1:]
        self.head = self.piece * self.blocks
        self.inner = self.heads * self.head
        self.pair = 2 * self.inner
        self.hidden = up_weight.shape[1]
        self.total = self.local * self.ctx
        self.half = self.rows // 2
        self.scale = 1.0 / math.sqrt(self.head)
        self.folded = self.ctx == 4
        self.direct = self.fsdp == 2 and self.shard % 16 == 0


def attention_kernel(z, order, masks, *refs):
    (meta, lengths), refs = refs[:2], refs[2:]
    count = z.blocks if z.direct else 1
    blocks, refs = refs[:count], refs[count:]
    own, refs = refs[0], refs[1:]
    pieces, refs = refs[: len(masks)], refs[len(masks) :]
    mixed, small, every, keys, query, probs, att, kept, sent = refs[:9]
    part = refs[9]
    row, col, lane = meta[0], meta[1], meta[2]
    if z.direct:
        places = block_places(z, order, row, col)
        total = jnp.zeros((TAIL, z.width), F32)
        for block, place in zip(blocks, places):
            mixed[aligned(place * z.shard, z.shard), :] = block[: z.shard, :]
            total = total + block[z.shard :, :].astype(F32)
        small[...] = total
    else:
        mixed[...] = blocks[0][: z.width, :]
        small[...] = blocks[0][z.width :, :].astype(F32)
    every[col] = own[...]
    share = z.rows // z.tp
    for at, step in enumerate(order):
        source = lax.rem(col - step + z.ctx, z.ctx)
        for which, mask in enumerate(masks):
            spot = jnp.bitwise_xor(lane, mask) * share
            every[source, aligned(spot, share), :] = pieces[which][at]
    b_q = jnp.where(lanes(0, z.inner, z.pair), small[7:8, : z.pair], 0.0)
    b_kv = jnp.where(lanes(z.inner, z.pair, z.pair), small[7:8, : z.pair], 0.0)

    @pl.loop(0, z.ctx)
    def _(at):
        both = dot(every[at], mixed[:, z.pair :], 1, 0) + b_kv
        both = both.astype(BF)
        for seq in range(z.seqs):
            piece = both[seq * z.local : (seq + 1) * z.local]
            keys[seq, aligned(at * z.local, z.local), :] = piece

    flat = dot(own[...], mixed[:, : z.pair], 1, 0) + b_q
    query[...] = jnp.where(lanes(0, z.inner, z.pair), flat, 0.0).astype(BF)
    docs = lengths.shape[1]
    key_at = lax.broadcasted_iota(jnp.int32, (1, z.total), 1)
    query_at = lax.broadcasted_iota(jnp.int32, (z.local, 1), 0) + col * z.local
    for seq in range(z.seqs):
        key_label = jnp.zeros((1, z.total), jnp.int32)
        query_label = jnp.zeros((z.local, 1), jnp.int32)
        end = 0
        for doc in range(docs):
            end = end + lengths[seq, doc]
            key_label = key_label + jnp.where(key_at >= end, 1, 0)
            query_label = query_label + jnp.where(query_at >= end, 1, 0)
        same = query_label == key_label
        flat = query[seq * z.local : (seq + 1) * z.local, :]
        result = jnp.zeros((z.local, z.pair), F32)
        for head in range(z.heads):
            low = head * z.head
            chosen = jnp.where(lanes(low, low + z.head, z.pair), flat, jnp.zeros_like(flat))
            scores = dot(chosen, keys[seq], 1, 1) * z.scale
            scores = jnp.where(same, scores, -1e30)
            weights = jnp.exp(scores - jnp.max(scores, axis=1, keepdims=True))
            chance = weights * (1.0 / jnp.sum(weights, axis=1, keepdims=True))
            chance = chance.astype(BF)
            probs[seq * z.heads + head] = chance
            low = low + z.inner
            found = dot(chance, keys[seq], 1, 0)
            result = jnp.where(lanes(low, low + z.head, z.pair), found, result)
        att[seq * z.local : (seq + 1) * z.local, :] = result.astype(BF)
    part[...] = dot(att[...], mixed[:, : z.pair], 1, 1)
    split_halves(z, lane, part, kept, sent)


def block_places(z, order, row, col):
    places = []
    for step in [0] + order:
        source = lax.rem(col - step + z.ctx, z.ctx)
        places.append(row * z.ctx + source)
        places.append((1 - row) * z.ctx + source)
    return places


def split_halves(z, lane, part, kept, sent):
    parity = jnp.bitwise_and(lane, 1)
    kept[...] = part[aligned(parity * z.half, z.half), :]
    sent[...] = part[aligned((1 - parity) * z.half, z.half), :].astype(sent.dtype)


def place_halves(z, lane, own, other, whole):
    parity = jnp.bitwise_and(lane, 1)
    whole[aligned(parity * z.half, z.half), :] = own[...].astype(F32)
    whole[aligned((1 - parity) * z.half, z.half), :] = other[...].astype(F32)


def forward_kernel(z, order, *refs):
    meta, own, other, rows, small = refs[:5]
    count = z.blocks if z.direct else 1
    blocks, refs = refs[5 : 5 + count], refs[5 + count :]
    up, down, normed_one, inverse_one, middle_b, slope, active, kept, sent, shown = refs[:10]
    work = refs[10]
    row, col, lane = meta[0], meta[1], meta[2]
    if z.direct:
        for block, place in zip(blocks, block_places(z, order, row, col)):
            up[aligned(place * z.shard, z.shard), :] = block[: z.shard, :]
            down[aligned(place * z.shard, z.shard), :] = block[z.shard :, :]
    else:
        up[...] = blocks[0][: z.width, :]
        down[...] = blocks[0][z.width :, :]
    place_halves(z, lane, own, other, work)
    hidden = rows[...].astype(F32) + work[...] + small[0:1, :]
    normed, inverse = norm_rows(hidden)
    normed_one[...] = normed
    inverse_one[...] = inverse
    middle_b[...] = (normed * small[1:2, :] + small[2:3, :]).astype(BF)
    pre = dot(middle_b[...], up[...], 1, 0) + small[6:7, :]
    activated, gradient = gelu_parts(pre)
    slope[...] = gradient
    active[...] = activated.astype(BF)
    show(z, row, middle_b, active, shown)
    work[...] = dot(active[...], down[...], 1, 1)
    split_halves(z, lane, work, kept, sent)


def show(z, row, columns, whole, shown):
    part = z.width // 2
    shown[:, :part] = half_columns(z, 1 - row, columns)
    shown[:, part:] = whole[...]


def half_columns(z, which, columns):
    part = z.width // 2
    return jnp.where(which == 0, columns[:, :part], columns[:, part:])


def middle_kernel(z, *refs):
    meta, own, other, normed_one, small, cotangent, up, down, slope = refs[:9]
    output, d_two, d_two_b, d_pre_b, kept, sent, sums, shown, work = refs[9:]
    lane = meta[2]
    place_halves(z, lane, own, other, work)
    middle = normed_one[...] * small[1:2, :] + small[2:3, :]
    normed, inverse = norm_rows(middle + work[...] + small[3:4, :])
    output[...] = (normed * small[4:5, :] + small[5:6, :]).astype(BF)
    grad_in = cotangent[...].astype(F32)
    sums[...] = jnp.zeros_like(sums)
    sums[4:5, :] = jnp.sum(grad_in * normed, axis=0, keepdims=True)
    sums[5:6, :] = jnp.sum(grad_in, axis=0, keepdims=True)
    d_res = norm_back(grad_in * small[4:5, :], normed, inverse)
    sums[3:4, :] = jnp.sum(d_res, axis=0, keepdims=True)
    d_two[...] = d_res
    d_two_b[...] = d_res.astype(BF)
    d_pre = dot(d_two_b[...], down[...], 1, 0) * slope[...]
    sums[6:7, :] = jnp.sum(d_pre, axis=0, keepdims=True)
    d_pre_b[...] = d_pre.astype(BF)
    show(z, meta[0], d_two_b, d_pre_b, shown)
    work[...] = dot(d_pre_b[...], up[...], 1, 1)
    split_halves(z, lane, work, kept, sent)


def second_grad_kernel(z, order, *refs):
    meta, middle_b, d_pre_b, d_two_b, active, acts, grads = refs[:7]
    outs, work = refs[7:-1], refs[-1]
    part = z.width // 2
    total = dot(half_columns(z, meta[0], middle_b), d_pre_b[...], 0, 0)
    total = total + dot(acts[:, :part], grads[:, part:], 0, 0)
    work[0] = total.astype(BF)
    total = dot(half_columns(z, meta[0], d_two_b), active[...], 0, 0)
    total = total + dot(grads[:, :part], acts[:, part:], 0, 0)
    work[1] = total.astype(BF)
    for start, out in zip(block_starts(z, order, meta[1]), outs):
        for at in range(2):
            out[at] = work[at, aligned(start, z.shard), :]


def second_grad_whole_kernel(*refs):
    _, middle_b, d_pre_b, d_two_b, active, out = refs
    out[0] = dot(middle_b[...], d_pre_b[...], 0, 0).astype(BF)
    out[1] = dot(d_two_b[...], active[...], 0, 0).astype(BF)


def backward_kernel(z, *refs):
    (meta, own, other, d_two, normed_one, inverse_one, small, mixed, att, query, keys), refs = (
        refs[:11],
        refs[11:],
    )
    (probs, sums_in), refs = refs[:2], refs[2:]
    d_one, d_one_b, d_query, d_keys, sums, kept, sent = refs[:7]
    work, grads, back = refs[7:]
    col, lane = meta[1], meta[2]
    place_halves(z, lane, own, other, work)
    d_middle = d_two[...] + work[...]
    normed = normed_one[...]
    sums[...] = sums_in[...]
    sums[1:2, :] = jnp.sum(d_middle * normed, axis=0, keepdims=True)
    sums[2:3, :] = jnp.sum(d_middle, axis=0, keepdims=True)
    d_res = norm_back(d_middle * small[1:2, :], normed, inverse_one[...])
    sums[0:1, :] = jnp.sum(d_res, axis=0, keepdims=True)
    d_one[...] = d_res
    d_one_b[...] = d_res.astype(BF)
    upper = lanes(z.inner, z.pair, z.pair)
    d_att = jnp.where(upper, dot(d_one_b[...], mixed[:, : z.pair], 1, 0), 0.0).astype(BF)
    qv_sum = jnp.zeros((1, z.pair), F32)
    for seq in range(z.seqs):
        span = slice(seq * z.local, (seq + 1) * z.local)
        d_here, a_here, q_here = d_att[span], att[span, :], query[span, :]
        product = d_here.astype(F32) * a_here.astype(F32)
        d_q = jnp.zeros((z.local, z.pair), F32)
        for head in range(z.heads):
            low = head * z.head
            near = lanes(low, low + z.head, z.pair)
            far = lanes(low + z.inner, low + z.inner + z.head, z.pair)
            q_head = jnp.where(near, q_here, jnp.zeros_like(q_here))
            d_head = jnp.where(far, d_here, jnp.zeros_like(d_here))
            delta = jnp.sum(jnp.where(far, product, 0.0), axis=1, keepdims=True)
            chance = probs[seq * z.heads + head]
            d_chance = dot(d_head, keys[seq], 1, 1)
            d_scores = (chance.astype(F32) * (d_chance - delta)).astype(BF)
            d_q = jnp.where(near, dot(d_scores, keys[seq], 1, 0), d_q)
            d_kv = dot(d_scores, q_head, 0, 0) * z.scale + dot(chance, d_head, 0, 0)
            if head == 0:
                grads[...] = d_kv
            else:
                grads[...] += d_kv
        d_q = d_q * z.scale
        qv_sum = qv_sum + jnp.sum(d_q, axis=0, keepdims=True)
        qv_sum = qv_sum + jnp.where(upper, jnp.sum(grads[...], axis=0, keepdims=True), 0.0)
        d_query[span, :] = d_q.astype(BF)
        for at in range(z.ctx):
            d_keys[at, span, :] = grads[at * z.local : (at + 1) * z.local, :].astype(BF)
    sums[7:8, : z.pair] = qv_sum
    for at in range(z.ctx):
        back[at] = dot(d_keys[at], mixed[:, z.pair :], 1, 1)
    back[col] += dot(d_query[...], mixed[:, : z.pair], 1, 1)
    parity = jnp.bitwise_and(lane, 1)
    kept[...] = back[:, aligned(parity * z.half, z.half), :]
    sent[...] = back[:, aligned((1 - parity) * z.half, z.half), :].astype(BF)


def first_grad_kernel(z, *refs):
    meta, rows, every, d_query, d_keys, d_one_b, att, sums = refs[:8]
    outs, work = refs[8:-1], refs[-1]
    near = dot(rows[...], d_query[...], 0, 0) + dot(d_one_b[...], att[...], 0, 0)
    work[:, : z.pair] = near.astype(BF)
    far = dot(every[0], d_keys[0], 0, 0)
    for at in range(1, z.ctx):
        far = far + dot(every[at], d_keys[at], 0, 0)
    work[:, z.pair :] = far.astype(BF)
    if len(outs) == 1:
        outs[0][...] = work[...]
        return
    part = z.width // 2
    for out, start in zip(outs, (meta[0] * part, (1 - meta[0]) * part)):
        out[:part, :] = work[aligned(start, part), :]
        out[part:, :] = sums[...].astype(BF)


def cut_kernel(z, meta, kept, got, near, far):
    chip = lax.shift_right_logical(meta[2], 1)
    size = z.half // 2
    for out, which in ((near, chip), (far, 1 - chip)):
        span = aligned(which * size, size)
        out[...] = (kept[:, span, :] + got[:, span, :].astype(F32)).astype(out.dtype)


def spread_kernel(z, order, meta, kept, got, own, *sends):
    for step, out in zip([0] + order, (own,) + sends):
        at = lax.rem(meta[1] + step, z.ctx)
        out[...] = (kept[at] + got[at].astype(F32)).astype(out.dtype)


def token_kernel(z, masks, meta, *refs):
    pieces, (d_one, out) = refs[:-2], refs[-2:]
    size = z.rows // z.tp
    for mask, piece in zip(masks, pieces):
        lane = jnp.bitwise_xor(meta[2], mask)
        start = jnp.bitwise_and(lane, 1) * z.half + lax.shift_right_logical(lane, 1) * size
        span = aligned(start, size)
        out[span, :] = (d_one[span, :] + piece[...].astype(F32)).astype(BF)


def where_equal(shape, left, right):
    rows = lax.broadcasted_iota(jnp.int32, shape, 0)
    cols = lax.broadcasted_iota(jnp.int32, shape, 1)
    return jnp.where(left(rows) == right(cols), 1.0, 0.0).astype(BF)


def same_head(z, heads, width):
    rows = lax.broadcasted_iota(jnp.int32, (heads, width), 0)
    cols = lax.broadcasted_iota(jnp.int32, (heads, width), 1)
    return (cols >= rows * z.head) & (cols < (rows + 1) * z.head)


def qv_lanes(z, head):
    start = lax.broadcasted_iota(jnp.int32, (2, z.width), 0) * z.inner + head * z.head
    cols = lax.broadcasted_iota(jnp.int32, (2, z.width), 1)
    return (cols >= start) & (cols < start + z.head)


def pack_kernel(z, *refs):
    meta, qkv, out, up_bias, qv_bias = refs[:5]
    vectors, pack = refs[5:-1], refs[-1]
    place = meta[0] * z.ctx + meta[1]
    inner = z.inner

    def spread(at):
        return where_equal((inner, z.width), lambda r: r + at * inner, lambda c: c)

    total = dot(qkv[0], spread(0), 1, 0) + dot(out[...], spread(1), 0, 0)
    total = total + dot(qkv[1], spread(2), 1, 0) + dot(qkv[2], spread(3), 1, 0)
    pack[: z.shard, :] = total.astype(BF)
    at = place * z.shard
    chosen = where_equal((z.shard, z.width), lambda r: r + at, lambda c: c)
    lines = [dot(vector[...], chosen, 1, 0) for vector in vectors]
    at = place * z.piece
    chosen = where_equal(
        (z.piece, z.width), lambda r: r + at, lambda c: jnp.bitwise_and(c, z.head - 1)
    )
    heads = up_bias.shape[1]
    wide = jnp.where(same_head(z, heads, z.width), dot(up_bias[...], chosen, 0, 0), 0.0)
    lines.append(jnp.sum(wide, axis=0, keepdims=True))
    line = jnp.zeros((1, z.width), F32)
    for head in range(z.heads):
        wide = jnp.where(qv_lanes(z, head), dot(qv_bias[head], chosen, 1, 0), 0.0)
        line = line + jnp.sum(wide, axis=0, keepdims=True)
    lines.append(line)
    pack[z.shard :, :] = jnp.concatenate(lines, axis=0).astype(BF)


def pack_plain(z, place, qkv_weight, out_weight, vectors, up_bias, qv_bias):
    vectors = lax.dynamic_update_slice(jnp.zeros((6, z.width), BF), vectors, (0, place * z.shard))
    up_row = lax.dynamic_update_slice(
        jnp.zeros((up_bias.shape[0], z.head), BF), up_bias, (0, place * z.piece)
    ).reshape(1, z.hidden)
    qv_row = lax.dynamic_update_slice(
        jnp.zeros((2, z.heads, z.head), BF), qv_bias, (0, 0, place * z.piece)
    ).reshape(1, z.pair)
    qv_row = jnp.pad(qv_row, ((0, 0), (0, z.width - z.pair)))
    tail = jnp.concatenate([vectors, up_row, qv_row], axis=0)
    mixed = jnp.concatenate([qkv_weight[0], out_weight.T, qkv_weight[1], qkv_weight[2]], axis=1)
    return mixed, tail


def terms(value):
    high = value.astype(BF)
    rest = value - high.astype(F32)
    middle = rest.astype(BF)
    return high, middle, (rest - middle.astype(F32)).astype(BF)


def exact_dot(left, right, over_left, over_right):
    if left.dtype == F32:
        return sum(dot(term, right, over_left, over_right) for term in terms(left))
    return sum(dot(left, term, over_left, over_right) for term in terms(right))


def finish_first_kernel(z, meta, *refs):
    blocks, refs = refs[: z.ctx], refs[z.ctx :]
    (g_qkv, g_out, g_up_bias, g_qv), g_vectors = refs[:4], refs[4:]
    total = blocks[0][...].astype(F32)
    for block in blocks[1:]:
        total = total + block[...].astype(F32)
    inner = z.inner
    for at, start in enumerate((0, 2 * inner, 3 * inner)):
        g_qkv[at] = total[: z.shard, start : start + inner]
    eye = where_equal((z.shard, z.shard), lambda r: r, lambda c: c)
    g_out[...] = exact_dot(total[: z.shard, inner : 2 * inner], eye, 0, 0)
    small = total[z.shard :]
    place = meta[0] * z.ctx + meta[1]
    at = place * z.shard
    chosen = where_equal((z.width, z.shard), lambda r: r, lambda c: c + at)
    found = exact_dot(small, chosen, 1, 0)
    for line, vector in enumerate(g_vectors):
        vector[...] = found[line : line + 1]
    at = place * z.piece
    chosen = where_equal(
        (z.width, z.piece), lambda r: jnp.bitwise_and(r, z.head - 1), lambda c: c + at
    )
    heads = g_up_bias.shape[1]
    wide = jnp.where(same_head(z, heads, z.width), small[6:7], 0.0)
    g_up_bias[...] = exact_dot(chosen, wide, 0, 1)
    wide = [jnp.where(qv_lanes(z, head), small[7:8], 0.0) for head in range(z.heads)]
    found = exact_dot(jnp.concatenate(wide, axis=0), chosen, 1, 0)
    for head in range(z.heads):
        g_qv[head] = found[2 * head : 2 * head + 2]


def finish_second_kernel(z, *refs):
    blocks, (g_up, g_down_t) = refs[: z.ctx], refs[z.ctx :]
    up, down = blocks[0][0].astype(F32), blocks[0][1].astype(F32)
    for block in blocks[1:]:
        up = up + block[0].astype(F32)
        down = down + block[1].astype(F32)
    g_up[...] = up
    g_down_t[...] = down


def share_kernel(z, order, *refs):
    meta, kept, got = refs[:3]
    outs, work = refs[3:-1], refs[-1]
    work[...] = (kept[...].astype(F32) + got[...].astype(F32)).astype(BF)
    for start, out in zip(block_starts(z, order, meta[1]), outs):
        out[: z.shard, :] = work[aligned(start, z.shard), :]
        out[z.shard :, :] = work[z.ctx * z.shard :, :]


def gather_blocks(order, shard):
    found = []
    for step in [0] + order:
        block = ring(shard, "ctx", step) if step else shard
        found += [block, ring(block, "fsdp", 1)]
    return found


def sum_rows(z, kept, sent):
    total = kept + flip(sent, "tp", 1).astype(F32)
    bit = 2
    while bit < z.tp:
        mine = total.astype(BF)
        total = mine.astype(F32) + flip(mine, "tp", bit).astype(F32)
        bit *= 2
    total = total.astype(BF)
    return total, flip(total, "tp", 1)


def reduce_shared(z, order, meta, kept, sent):
    got = ring(sent, "fsdp", 1)
    shape = kept.shape[:-2] + (kept.shape[-2] - (z.ctx - 1) * z.shard, kept.shape[-1])
    pieces = call(
        functools.partial(share_kernel, z, order),
        [(shape, BF)] * (z.ctx + z.folded),
        (kept, got),
        smem=(meta,),
        scratch=[pltpu.VMEM(kept.shape, BF)],
    )
    return send_pieces(z, order, pieces)


def send_pieces(z, order, pieces):
    if not z.folded:
        return [pieces[0]] + [ring(piece, "ctx", step) for step, piece in zip(order, pieces[1:])]
    own, right, left, far, fold = pieces
    fold = lax.ppermute(fold, "ctx", ((0, 1), (3, 2)))
    right = lax.ppermute(right, "ctx", ((0, 1), (1, 2), (2, 3)))
    left = lax.ppermute(left, "ctx", ((1, 0), (2, 1), (3, 2)))
    far = (far.astype(F32) + fold.astype(F32)).astype(BF)
    return [own, right, left, ring(far, "ctx", 2)]


def block_starts(z, order, col):
    starts = [lax.rem(col + step, z.ctx) for step in [0] + order]
    if z.folded:
        starts.append(jnp.where(col == 0, z.ctx - 1, 0))
    return [start * z.shard for start in starts]


def body(
    tokens,
    lengths,
    qkv_weight,
    qv_bias,
    out_weight,
    out_bias,
    norm1_gain,
    norm1_bias,
    up_weight,
    up_bias,
    down_weight,
    down_bias,
    norm2_gain,
    norm2_bias,
    cotangent,
):
    z = Sizes(tokens, qv_bias, up_weight)
    rows = tokens.reshape(-1, z.width)
    row, col, lane = (lax.axis_index(a).astype(jnp.int32) for a in ("fsdp", "ctx", "tp"))
    meta = jnp.stack([row, col, lane])
    place = row * z.ctx + col
    order = near_first(z.ctx)
    full = (z.rows, z.width)
    half = (z.half, z.width)
    square = (z.width, z.width)

    vectors = (out_bias, norm1_gain, norm1_bias, down_bias, norm2_gain, norm2_bias)
    if z.direct:
        (first_pack,) = call(
            functools.partial(pack_kernel, z),
            [((z.shard + TAIL, z.width), BF)],
            (
                qkv_weight,
                out_weight,
                up_bias.T,
                qv_bias.transpose(1, 0, 2),
                *(vector.reshape(1, z.shard) for vector in vectors),
            ),
            smem=(meta,),
            spare=58 << 20,
        )
    else:
        mixed_shard, tail = pack_plain(
            z, place, qkv_weight, out_weight, jnp.stack(vectors), up_bias, qv_bias
        )
    share = z.rows // z.tp
    token_share = lax.dynamic_slice_in_dim(rows, lane * share, share, 0)
    got = jnp.stack([ring(token_share, "ctx", step) for step in order])
    pieces, masks = [got], [0]
    bit = z.tp // 2
    while bit:
        pieces = pieces + [flip(piece, "tp", bit) for piece in pieces]
        masks = masks + [mask ^ bit for mask in masks]
        bit //= 2
    second_pack = jnp.concatenate([up_weight, down_weight.T], axis=0)
    if z.direct:
        first_blocks = gather_blocks(order, first_pack)
        second_blocks = gather_blocks(order, second_pack)
    else:
        split = ("fsdp", "ctx")
        mixed_all = lax.all_gather(mixed_shard, split, axis=0, tiled=True)
        tail_all = jnp.sum(lax.all_gather(tail, split, axis=0).astype(F32), axis=0).astype(BF)
        first_blocks = [jnp.concatenate([mixed_all, tail_all], axis=0)]
        second_all = lax.all_gather(second_pack, split, axis=0)
        second_all = second_all.reshape(z.blocks, 2, z.shard, z.hidden).transpose(1, 0, 2, 3)
        second_blocks = [second_all.reshape(2 * z.width, z.hidden)]

    mixed, small, every, keys, query, probs, att, kept, sent = call(
        functools.partial(attention_kernel, z, order, masks),
        [
            (square, BF),
            ((TAIL, z.width), F32),
            ((z.ctx,) + full, BF),
            ((z.seqs, z.total, z.pair), BF),
            ((z.rows, z.pair), BF),
            ((z.seqs * z.heads, z.local, z.total), BF),
            ((z.rows, z.pair), BF),
            (half, F32),
            (half, BF),
        ],
        (*first_blocks, rows, *pieces),
        smem=(meta, lengths),
        scratch=[pltpu.VMEM(full, F32)],
        flops=4 * z.rows * z.ctx * z.width * z.pair,
    )
    own, other = sum_rows(z, kept, sent)
    shown = ((z.rows, z.width // 2 + z.hidden), BF)
    up, down, normed_one, inverse_one, middle_b, slope, active, kept, sent, acts = call(
        functools.partial(forward_kernel, z, order),
        [
            (square, BF),
            (square, BF),
            (full, F32),
            ((z.rows, 1), F32),
            (full, BF),
            (full, F32),
            (full, BF),
            (half, F32),
            (half, BF),
            shown,
        ],
        (own, other, rows, small, *second_blocks),
        smem=(meta,),
        scratch=[pltpu.VMEM(full, F32)],
        flops=4 * z.rows * z.width * z.hidden,
    )
    own, other = sum_rows(z, kept, sent)
    output, d_two, d_two_b, d_pre_b, kept, sent, sums, grads = call(
        functools.partial(middle_kernel, z),
        [
            (full, BF),
            (full, F32),
            (full, BF),
            (full, BF),
            (half, F32),
            (half, BF),
            ((TAIL, z.width), F32),
            shown,
        ],
        (own, other, normed_one, small, cotangent.reshape(full), up, down, slope),
        smem=(meta,),
        scratch=[pltpu.VMEM(full, F32)],
        flops=4 * z.rows * z.width * z.hidden,
    )
    grad_args = (middle_b, d_pre_b, d_two_b, active)
    grad_flops = 4 * z.rows * z.width * z.hidden
    if z.direct:
        acts = ring(acts, "fsdp", 1)
        grads = ring(grads, "fsdp", 1)
        second = call(
            functools.partial(second_grad_kernel, z, order),
            [((2, z.shard, z.hidden), BF)] * (z.ctx + z.folded),
            (*grad_args, acts, grads),
            smem=(meta,),
            scratch=[pltpu.VMEM((2, z.width // 2, z.hidden), BF)],
            flops=grad_flops,
        )
        second = send_pieces(z, order, second)
    else:
        (second_grads,) = call(
            second_grad_whole_kernel,
            [((2,) + square, BF)],
            grad_args,
            smem=(meta,),
            flops=grad_flops,
        )
    own, other = sum_rows(z, kept, sent)
    terms_of = (z.ctx, z.half, z.width)
    d_one, d_one_b, d_query, d_keys, sums, kept, sent = call(
        functools.partial(backward_kernel, z),
        [
            (full, F32),
            (full, BF),
            ((z.rows, z.pair), BF),
            ((z.ctx, z.rows, z.pair), BF),
            ((TAIL, z.width), F32),
            (terms_of, F32),
            (terms_of, BF),
        ],
        (own, other, d_two, normed_one, inverse_one, small, mixed, att, query, keys, probs, sums),
        smem=(meta,),
        scratch=[
            pltpu.VMEM(full, F32),
            pltpu.VMEM((z.total, z.pair), F32),
            pltpu.VMEM((z.ctx,) + full, F32),
        ],
        flops=10 * z.rows * z.heads * z.total * z.pair,
    )
    terms_of = (z.ctx, z.half // 2, z.width)
    near, far = call(
        functools.partial(cut_kernel, z),
        [(terms_of, F32), (terms_of, BF)],
        (kept, flip(sent, "tp", 1)),
        smem=(meta,),
    )
    quarter = terms_of[1:]
    total, *sends = call(
        functools.partial(spread_kernel, z, order),
        [(quarter, F32)] + [(quarter, BF)] * (z.ctx - 1),
        (near, flip(far, "tp", 2)),
        smem=(meta,),
    )
    for step, piece in zip(order, sends):
        total = total + ring(piece, "ctx", step).astype(F32)
    total = total.astype(BF)
    backs = [total, flip(total, "tp", 2)]
    backs += [flip(piece, "tp", 1) for piece in backs]
    if z.direct:
        part = (z.width // 2 + TAIL, z.width)
        grad_outs = [(part, BF), (part, BF)]
    else:
        grad_outs = [(square, BF)]
    first_parts = call(
        functools.partial(first_grad_kernel, z),
        grad_outs,
        (rows, every, d_query, d_keys, d_one_b, att, sums),
        smem=(meta,),
        scratch=[pltpu.VMEM(square, BF)],
        flops=2 * z.rows * (z.ctx + 2) * z.width * z.pair,
    )
    (token_grad,) = call(
        functools.partial(token_kernel, z, [0, 2, 1, 3]),
        [(full, BF)],
        (*backs, d_one),
        smem=(meta,),
    )

    if z.direct:
        first = reduce_shared(z, order, meta, *first_parts)
        g_up, g_down_t = call(
            functools.partial(finish_second_kernel, z),
            [(up_weight.shape, F32), (up_weight.shape, F32)],
            second,
        )
        g_down = g_down_t.T
        g_qkv, g_out, g_up_bias, g_qv, *g_vectors = call(
            functools.partial(finish_first_kernel, z),
            [
                (qkv_weight.shape, F32),
                (out_weight.shape, F32),
                (up_bias.shape[::-1], F32),
                ((z.heads, 2, z.piece), F32),
            ]
            + [((1, z.shard), F32)] * 6,
            first,
            smem=(meta,),
        )
        g_up_bias = g_up_bias.T
        g_qv = g_qv.transpose(1, 0, 2)
        g_vectors = [vector.reshape(z.shard) for vector in g_vectors]
    else:
        split = ("fsdp", "ctx")
        second = lax.psum_scatter(
            second_grads.astype(F32), split, scatter_dimension=1, tiled=True
        )
        g_up, g_down = second[0], second[1].T
        g_mixed = lax.psum_scatter(
            first_parts[0].astype(F32), split, scatter_dimension=0, tiled=True
        )
        g_small = lax.psum(sums, split)
        inner = z.inner
        starts = (0, 2 * inner, 3 * inner)
        g_qkv = jnp.stack([g_mixed[:, start : start + inner] for start in starts])
        g_out = g_mixed[:, inner : 2 * inner].T
        g_vectors = lax.dynamic_slice(g_small, (0, place * z.shard), (6, z.shard))
        g_up_bias = lax.dynamic_slice(
            g_small[6].reshape(up_bias.shape[0], z.head), (0, place * z.piece), up_bias.shape
        )
        g_qv = lax.dynamic_slice(
            g_small[7, : z.pair].reshape(2, z.heads, z.head),
            (0, 0, place * z.piece),
            qv_bias.shape,
        )
    return (
        output.reshape(tokens.shape),
        token_grad.reshape(tokens.shape),
        g_qkv,
        g_qv,
        g_out,
        g_vectors[0],
        g_vectors[1],
        g_vectors[2],
        g_up,
        g_up_bias,
        g_down,
        g_vectors[3],
        g_vectors[4],
        g_vectors[5],
    )


def solution(mesh):
    split = ("fsdp", "ctx")
    vector = P(split)
    rows = P("fsdp", "ctx", None)
    weights = (
        P(None, split, "tp"),
        P(None, "tp", split),
        P("tp", split),
        vector,
        vector,
        vector,
        P(split, "tp"),
        P("tp", split),
        P("tp", split),
        vector,
        vector,
        vector,
    )

    return jax.shard_map(
        body,
        mesh=mesh,
        in_specs=(rows, P("fsdp", None)) + weights + (rows,),
        out_specs=(rows, rows) + weights,
        check_vma=False,
    )
```
